32 devices in a mesh: groups: 2 (over y), feat: 4 (over z), pts: 2 (over x), sub: 2 (over core).
Axes of the slice: x: 2, y: 2, z: 4, core: 2. Of those that a mesh axis runs over, the one named last changes fastest.
Arguments:
- points: bfloat16 [256, 256], P(('groups', 'pts')), parts along dimension 0, may hold values from -6 to 6
- freqs: bfloat16 [256, 65536], P(None, ('feat', 'sub')), may hold values from -0.75 to 0.75
- phases: float32 [65536], P(('feat', 'sub')), may hold values from 0 to 6.283
- basis: bfloat16 [131072, 1024], P(('groups', 'feat', 'sub'), 'pts'), parts along dimension 0, may hold values from -0.0203125 to 0.0203125
Outputs:
- coefs: float32 [2048, 128], P('groups', 'pts'), parts along dimension 0
- new_basis: float32 [131072, 128], P(('groups', 'feat', 'sub'), 'pts'), parts along dimension 0
- factor: float32 [256, 128], P(('groups', 'pts')), parts along dimension 0
The draws below stay inside these ranges and needn't reach their ends.
There are 2 independent parts, one for each index of `groups`. The reference program is written for one: setup_inputs(seed, part) draws one part's arguments, and reference() takes and returns one part's arrays. A program takes and returns all parts, laid end to end along the dimension named above; an argument that names none is the same for every part. Nothing has to cross between parts.
All inputs are finite; a program needn't handle non-finite values.
Results may differ from the reference program's by a relative error of at most 0.00055.
Values may be sent and summed in bfloat16 or wider, within the bound.
No kernel may reach another device: no remote copies, remote signals or barrier semaphores. Data moves between devices by JAX's collectives and lax.ppermute only.
A program may use at most 128 MiB of HBM per device.

```python
import jax
import jax.numpy as jnp
from jax import lax

DIMS = 256
FEATS = 65536
RANK = 1024
POINTS = 128


def draw_basis(key, part):
    key_own = jax.random.fold_in(key, 11)
    key_common = jax.random.fold_in(key, 12)
    scale = 1.0 / jnp.sqrt(jnp.float32(FEATS))
    own = jnp.clip(jax.random.normal(key_own, (FEATS, RANK), jnp.float32), -4.0, 4.0)
    common = jnp.clip(jax.random.normal(key_common, (FEATS, 1), jnp.float32), -4.0, 4.0)
    return ((own + 0.3 * common) * scale).astype(jnp.bfloat16)


def level_of(own_key, extent, pieces, smallest, high):
    def one(position, blocks):
        heights = jax.random.uniform(jax.random.fold_in(jax.random.fold_in(own_key, 6), position), (blocks,), jnp.float32, smallest / len(pieces), high / len(pieces))
        return jnp.repeat(jnp.exp(heights), extent[position] // blocks).reshape((-1,) + (1,) * (len(extent) - position - 1))

    loudness = one(*pieces[0])
    for cut in pieces[1:]:
        loudness = loudness * one(*cut)
    return loudness


def noise(own_key, extent, scale, limit, pieces=(), kind=jnp.bfloat16):
    entries = scale * jax.random.normal(own_key, extent, jnp.float32)
    if pieces:
        entries = entries * level_of(own_key, extent, pieces, -0.22, 0.18)
    return jnp.clip(entries, -limit, limit).astype(kind)


def setup_inputs(seed: int = 0, part: int = 0) -> dict:
    arg_keys = jax.random.split(jax.random.key(seed), 5)
    part_splits = jax.random.split(jax.random.fold_in(arg_keys[4], part), 5)
    points = noise(part_splits[0], (POINTS, DIMS), 1.0, 6.0, ((0, 2),))
    freqs = noise(arg_keys[1], (DIMS, FEATS), 0.125, 0.75, ((1, 8),))
    phases = jnp.clip(6.283 * jax.random.uniform(arg_keys[2], (FEATS,), jnp.float32) ** level_of(arg_keys[2], (FEATS,), ((0, 8),), -0.2, 0.2), 0.0, 6.283)
    basis = draw_basis(jax.random.fold_in(jax.random.fold_in(arg_keys[4], part), 71), part)
    return {"points": points, "freqs": freqs, "phases": phases, "basis": basis}


def reference(points, freqs, phases, basis):
    highest = lax.Precision.HIGHEST
    phase_in = jnp.dot(points.astype(jnp.float32), freqs.astype(jnp.float32), preferred_element_type=jnp.float32)
    features = jnp.cos(phase_in + phases[None, :]).T
    basis_f = basis.astype(jnp.float32)
    coefs = jnp.dot(basis_f.T, features, precision=highest)
    fitted = jnp.dot(basis_f, coefs, precision=highest)
    residual = features - fitted
    gram = jnp.dot(residual.T, residual, precision=highest) / FEATS
    factor = jnp.linalg.cholesky(gram)
    eye_mat = jnp.eye(POINTS, dtype=jnp.float32)
    inverse = jax.scipy.linalg.solve_triangular(factor, eye_mat, lower=True)
    new_basis = jnp.dot(residual, inverse.T, precision=highest)
    return (coefs, new_basis, factor)
```

```python
import functools

import jax
import jax.numpy as jnp
from jax import lax
from jax.experimental import pallas as pl
from jax.experimental.pallas import tpu as pltpu
from jax.sharding import PartitionSpec as P

BF16, F32, WIRE = jnp.bfloat16, jnp.float32, jnp.float16

COS = (
    0.9999999889369959,
    -0.4999998901135819,
    0.041666488148010265,
    -0.0013887798934755957,
    2.4769791619676175e-05,
    -2.7078195310289617e-07,
    1.7242244242579268e-09,
)
TURN_HEAD = 6.28125
TURN_REST = 0.0019353071795864769


def cosine(x):
    turns = jnp.round(x * 0.15915494309189535)
    x = (x - turns * TURN_HEAD) - turns * TURN_REST
    t = x * x
    y = COS[-1]
    for c in COS[-2::-1]:
        y = y * t + c
    return y


def split(x):
    high = x.astype(BF16)
    return high, (x - high.astype(F32)).astype(BF16)


def dot_nt(a, b):
    return lax.dot_general(a, b, (((1,), (1,)), ((), ())), preferred_element_type=F32)


def estimate(flops, moved):
    return pl.CostEstimate(flops=int(flops), bytes_accessed=int(moved), transcendentals=0)


def coef_kernel(place, points, freqs, phases, basis, feats, keep, send, total):
    step = pl.program_id(0)
    count = points.shape[0]
    half = keep.shape[0]
    x = jnp.dot(points[...], freqs[...], preferred_element_type=F32) + phases[...]
    value = cosine(x)
    feats[...] = value
    both = jnp.concatenate(split(value), axis=0)
    part = jnp.dot(both, basis[...], preferred_element_type=F32)
    part = part[:count] + part[count:]

    @pl.when(step == 0)
    def _():
        total[...] = part

    @pl.when(step > 0)
    def _():
        total[...] += part

    @pl.when(step == pl.num_programs(0) - 1)
    def _():
        sub = place[1]
        keep[...] = total[pl.ds(pl.multiple_of(sub * half, half), half), :]
        send[...] = total[pl.ds(pl.multiple_of((1 - sub) * half, half), half), :]


def partial_coefs(place, points, freqs, phases, basis, block=1024):
    count, dims = points.shape
    width, rank = basis.shape
    half = count // 2
    return pl.pallas_call(
        coef_kernel,
        grid_spec=pltpu.PrefetchScalarGridSpec(
            num_scalar_prefetch=1,
            grid=(width // block,),
            in_specs=[
                pl.BlockSpec((count, dims), lambda i, p: (0, 0)),
                pl.BlockSpec((dims, block), lambda i, p: (0, i)),
                pl.BlockSpec((1, block), lambda i, p: (0, i)),
                pl.BlockSpec((block, rank), lambda i, p: (i, 0)),
            ],
            out_specs=[
                pl.BlockSpec((count, block), lambda i, p: (0, i)),
                pl.BlockSpec((half, rank), lambda i, p: (0, 0)),
                pl.BlockSpec((half, rank), lambda i, p: (0, 0)),
            ],
            scratch_shapes=[pltpu.VMEM((count, rank), F32)],
        ),
        out_shape=[
            jax.ShapeDtypeStruct((count, width), F32),
            jax.ShapeDtypeStruct((half, rank), F32),
            jax.ShapeDtypeStruct((half, rank), F32),
        ],
        cost_estimate=estimate(
            2 * count * width * (dims + 2 * rank), width * (2 * dims + 2 * rank + 4 * count)
        ),
        name="coefs",
    )(place, points, freqs, phases, basis)


def fit_kernel(flip, place, own_a, got_a, own_b, got_b, feats_a, feats_b, basis, left, fit, coef_a, coef_b, parts):
    step = pl.program_id(0)
    half, rank = own_a.shape
    count = 4 * half

    @pl.when(step == 0)
    def _():
        sub = place[1]
        for base, own, got, coef in ((0, own_a, got_a, coef_a), (2 * half, own_b, got_b, coef_b)):
            mine = pl.ds(pl.multiple_of(sub * half, half), half)
            other = pl.ds(pl.multiple_of((1 - sub) * half, half), half)
            coef[mine, :] = own[...]
            coef[other, :] = got[...]
            high, low = split(coef[...])
            parts[base : base + 2 * half, :] = high
            parts[count + base : count + base + 2 * half, :] = low

    value = dot_nt(parts[...], basis[...])
    value = value[:count] + value[count:]
    fit[...] = value
    left[: 2 * half, :] = feats_a[...] - value[: 2 * half]
    left[2 * half :, :] = feats_b[...] - value[2 * half :]


def fitted(place, coefs, feats_a, feats_b, basis, flip, block=1024):
    half, rank = coefs[0].shape
    count = 4 * half
    width = basis.shape[0]
    blocks = width // 2 // block

    def at(i, p):
        side = 1 - p[0] if flip else p[0]
        return side * blocks + i

    small = pl.BlockSpec((half, rank), lambda i, p: (0, 0))
    return pl.pallas_call(
        functools.partial(fit_kernel, flip),
        grid_spec=pltpu.PrefetchScalarGridSpec(
            num_scalar_prefetch=1,
            grid=(blocks,),
            in_specs=[
                small,
                small,
                small,
                small,
                pl.BlockSpec((2 * half, block), lambda i, p: (0, at(i, p))),
                pl.BlockSpec((2 * half, block), lambda i, p: (0, at(i, p))),
                pl.BlockSpec((block, rank), lambda i, p: (at(i, p), 0)),
            ],
            out_specs=[
                pl.BlockSpec((count, block), lambda i, p: (0, i)),
                pl.BlockSpec((count, block), lambda i, p: (0, i)),
                pl.BlockSpec((2 * half, rank), lambda i, p: (0, 0)),
                pl.BlockSpec((2 * half, rank), lambda i, p: (0, 0)),
            ],
            scratch_shapes=[pltpu.VMEM((2 * count, rank), BF16)],
        ),
        out_shape=[
            jax.ShapeDtypeStruct((count, width // 2), F32),
            jax.ShapeDtypeStruct((count, width // 2), F32),
            jax.ShapeDtypeStruct((2 * half, rank), F32),
            jax.ShapeDtypeStruct((2 * half, rank), F32),
        ],
        cost_estimate=estimate(2 * count * width * rank, width * (rank + 6 * count)),
        name="fit",
    )(place, *coefs, feats_a, feats_b, basis)


def gram_kernel(place, resid, keep, send, total):
    step = pl.program_id(0)
    count = resid.shape[0]
    half = count // 2
    both = jnp.concatenate(split(resid[...]), axis=0)
    part = dot_nt(both, both)
    part = (part[:count, :count] + part[count:, count:]) + (part[:count, count:] + part[count:, :count])

    @pl.when(step == 0)
    def _():
        total[...] = part

    @pl.when(step > 0)
    def _():
        total[...] += part

    @pl.when(step == pl.num_programs(0) - 1)
    def _():
        sub = place[1]
        own = place[0] == 0

        def rows(start):
            value = total[pl.ds(pl.multiple_of(start * half, half), half), :]
            swapped = jnp.concatenate([value[:, half:], value[:, :half]], axis=1)
            return jnp.where(own, value, swapped)

        mine = jnp.where(own, sub, 1 - sub)
        keep[...] = rows(mine)
        send[...] = rows(1 - mine)


def partial_gram(place, resid, block=1024):
    count, width = resid.shape
    half = count // 2
    return pl.pallas_call(
        gram_kernel,
        grid_spec=pltpu.PrefetchScalarGridSpec(
            num_scalar_prefetch=1,
            grid=(width // block,),
            in_specs=[pl.BlockSpec((count, block), lambda i, p: (0, i))],
            out_specs=[
                pl.BlockSpec((half, count), lambda i, p: (0, 0)),
                pl.BlockSpec((half, count), lambda i, p: (0, 0)),
            ],
            scratch_shapes=[pltpu.VMEM((count, count), F32)],
        ),
        out_shape=[jax.ShapeDtypeStruct((half, count), F32)] * 2,
        cost_estimate=estimate(8 * count * count * width, 4 * width * count),
        name="gram",
    )(place, resid)


def basis_kernel(place, weights, mine, theirs, out):
    first = pl.program_id(0) < pl.num_programs(0) // 2

    @pl.when(first)
    def _():
        out[...] = finish(weights[...], mine[...])

    @pl.when(jnp.logical_not(first))
    def _():
        out[...] = finish(weights[...], theirs[...])


def finish(weights, resid):
    high, low = split(weights)
    lhs = jnp.concatenate(
        [jnp.concatenate([high, high], axis=1), jnp.concatenate([low, low], axis=1)], axis=0
    )
    value = jnp.dot(lhs, jnp.concatenate(split(resid), axis=0), preferred_element_type=F32)
    rows = weights.shape[0]
    return value[:rows] + value[rows:]


def new_rows(place, weights, mine, theirs, block=1024):
    rows, count = weights.shape
    half_width = mine.shape[1]
    blocks = half_width // block
    return pl.pallas_call(
        basis_kernel,
        grid_spec=pltpu.PrefetchScalarGridSpec(
            num_scalar_prefetch=1,
            grid=(2 * blocks,),
            in_specs=[
                pl.BlockSpec((rows, count), lambda i, p: (0, 0)),
                pl.BlockSpec((count, block), lambda i, p: (0, jnp.minimum(i, blocks - 1))),
                pl.BlockSpec((count, block), lambda i, p: (0, jnp.maximum(i - blocks, 0))),
            ],
            out_specs=pl.BlockSpec(
                (rows, block),
                lambda i, p: (0, jnp.where(i < blocks, p[0], 1 - p[0]) * blocks + lax.rem(i, blocks)),
            ),
        ),
        out_shape=jax.ShapeDtypeStruct((rows, 2 * half_width), F32),
        cost_estimate=estimate(8 * rows * count * 2 * half_width, 4 * half_width * (2 * count + 2 * rows)),
        name="new_basis",
    )(place, weights, mine, theirs)


def swap(x, axis):
    return lax.ppermute(x, axis, [(0, 1), (1, 0)])


def sum_over(x, axis, size):
    terms = [x] + [lax.ppermute(x, axis, [(i, i ^ m) for i in range(size)]) for m in range(1, size)]
    while len(terms) > 1:
        terms = [a + b for a, b in zip(terms[::2], terms[1::2])]
    return terms[0]


def paired(feat, feats_total, points, freqs, phases, basis):
    count = points.shape[0]
    place = jnp.stack([lax.axis_index("pts"), lax.axis_index("sub")]).astype(jnp.int32)
    phases = phases[None, :]
    others = swap(points, "pts")
    feats, coefs = [], []
    for chunk in (points, others):
        values, keep, send = partial_coefs(place, chunk, freqs, phases, basis)
        own = sum_over(keep + swap(send, "sub"), "feat", feat)
        feats.append(values)
        coefs += [own, swap(own, "sub")]

    left_far, fit_far, coef_a, coef_b = fitted(place, coefs, *feats, basis, 1)
    left_near, fit_near, _, _ = fitted(place, coefs, *feats, basis, 0)

    def received(left, fit):
        got = swap(fit.astype(WIRE), "pts").astype(F32)
        return left - jnp.concatenate([got[count:], got[:count]], axis=0)

    near = received(left_near, fit_far)
    keep, send = partial_gram(place, near)
    gram = keep + swap(send, "sub")
    gram = gram + swap(gram, "pts")
    gram = sum_over(gram, "feat", feat)
    far_gram = swap(gram, "sub")
    first = lax.axis_index("sub") == 0
    gram = jnp.where(
        first, jnp.concatenate([gram, far_gram], 0), jnp.concatenate([far_gram, gram], 0)
    ) / feats_total
    factor = jnp.linalg.cholesky(gram)
    inverse = jax.scipy.linalg.solve_triangular(factor, jnp.eye(2 * count, dtype=F32), lower=True)

    start = lax.axis_index("pts") * count
    factor_rows = lax.dynamic_slice_in_dim(factor, start, count, 0)
    weights = lax.dynamic_slice_in_dim(inverse, start, count, 0)
    swapped = jnp.concatenate([weights[:, count:], weights[:, :count]], axis=1)
    weights = jnp.where(lax.axis_index("pts") == 0, weights, swapped)
    far = received(left_far, fit_near)
    new_basis = new_rows(place, weights, near, far)

    got = swap(coef_b, "pts")
    coefs = jnp.where(
        lax.axis_index("pts") == 0,
        jnp.concatenate([coef_a, got], axis=1),
        jnp.concatenate([got, coef_a], axis=1),
    )
    return coefs.T, new_basis.T, factor_rows


def general(feats_total, points, freqs, phases, basis):
    highest = lax.Precision.HIGHEST
    phase_in = jnp.einsum("pd,df->fp", points, freqs, preferred_element_type=F32)
    features = jnp.cos(phase_in + phases[:, None])
    point_cols = features.shape[1]
    whole_basis = lax.all_gather(basis, "pts", axis=1, tiled=True).astype(F32)
    partial_value = jnp.einsum("fk,fp->kp", whole_basis, features, precision=highest)
    coefs = lax.psum(partial_value, ("feat", "sub"))
    residual = features - jnp.dot(whole_basis, coefs, precision=highest)
    spread = lax.all_gather(residual, "pts", axis=1, tiled=True)
    block = jnp.einsum("fq,fp->qp", spread, residual, precision=highest)
    total_pts = block.shape[0]
    block = lax.psum(block, ("feat", "sub")) / feats_total
    gram = lax.all_gather(block, "pts", axis=1, tiled=True)
    factor = jnp.linalg.cholesky(gram)
    inverse = jax.scipy.linalg.solve_triangular(factor, jnp.eye(total_pts, dtype=F32), lower=True)
    offset = lax.axis_index("pts") * point_cols
    factor_rows = lax.dynamic_slice_in_dim(factor, offset, point_cols, 0)
    inv_rows = lax.dynamic_slice_in_dim(inverse, offset, point_cols, 0)
    new_basis = jnp.einsum("fq,pq->fp", spread, inv_rows, precision=highest)
    return coefs, new_basis, factor_rows


def solution(mesh):
    sizes = dict(mesh.shape)
    feat, pts, sub = sizes["feat"], sizes["pts"], sizes["sub"]

    def on_device(points, freqs, phases, basis):
        feats_total = phases.shape[0] * feat * sub
        if pts == 2 and sub == 2 and feat in (1, 2, 4, 8):
            return paired(feat, feats_total, points, freqs, phases, basis)
        return general(feats_total, points, freqs, phases, basis)

    return jax.shard_map(
        on_device,
        mesh=mesh,
        in_specs=(
            P(("groups", "pts"), None),
            P(None, ("feat", "sub")),
            P(("feat", "sub")),
            P(("groups", "feat", "sub"), "pts"),
        ),
        out_specs=(
            P("groups", "pts"),
            P(("groups", "feat", "sub"), "pts"),
            P(("groups", "pts"), None),
        ),
        check_vma=False,
    )
```

```python
import functools

import jax
import jax.numpy as jnp
from jax import lax
from jax.experimental import pallas as pl
from jax.experimental.pallas import tpu as pltpu
from jax.sharding import PartitionSpec as P

BF16, F32, WIRE = jnp.bfloat16, jnp.float32, jnp.float16

COS = (
    0.9999999889369959,
    -0.4999998901135819,
    0.041666488148010265,
    -0.0013887798934755957,
    2.4769791619676175e-05,
    -2.7078195310289617e-07,
    1.7242244242579268e-09,
)
TURN_HEAD = 6.28125
TURN_REST = 0.0019353071795864769


def cosine(x):
    turns = jnp.round(x * 0.15915494309189535)
    x = (x - turns * TURN_HEAD) - turns * TURN_REST
    t = x * x
    y = COS[-1]
    for c in COS[-2::-1]:
        y = y * t + c
    return y


def split(x):
    high = x.astype(BF16)
    return high, (x - high.astype(F32)).astype(BF16)


def dot_nt(a, b):
    return lax.dot_general(a, b, (((1,), (1,)), ((), ())), preferred_element_type=F32)


LONG = pl.CostEstimate(flops=1000, bytes_accessed=20_000_000, transcendentals=0)
COST = pl.CostEstimate(flops=1000, bytes_accessed=1000, transcendentals=0)


def on_chip(kernel, name, out_shape, scalars=0, cost=COST, **extra):
    out_shape = [jax.ShapeDtypeStruct(*out) for out in out_shape]
    vmem = pl.BlockSpec(memory_space=pltpu.VMEM)
    smem = pl.BlockSpec(memory_space=pltpu.SMEM)

    def call(*args):
        return pl.pallas_call(
            kernel,
            in_specs=[smem] * scalars + [vmem] * (len(args) - scalars),
            out_specs=[vmem] * len(out_shape),
            out_shape=out_shape,
            cost_estimate=cost,
            compiler_params=pltpu.CompilerParams(vmem_limit_bytes=16 << 20),
            name=name,
            **extra,
        )(*args)

    return call


def half_rows(index, half):
    return pl.ds(pl.multiple_of(index * half, half), half)


def make_features(points, freqs, phases, feats, parts, at):
    count = points.shape[0]
    x = jnp.dot(points[...], freqs[:, at], preferred_element_type=F32) + phases[:, at]
    value = cosine(x)
    feats[:, at] = value
    parts[:count, at], parts[count:, at] = split(value)


def own_coefs(points, freqs, phases, basis, block=1024):
    count, width, rank = points.shape[0], freqs.shape[1], basis.shape[1]
    blocks = width // block
    spans = [pl.ds(i * block, block) for i in range(blocks)]

    def kernel(points, freqs, phases, basis, feats, coefs, freqs_in, phases_in, basis_in, points_in, parts, sems):
        first = [
            pltpu.make_async_copy(points, points_in, sems.at[0]),
            pltpu.make_async_copy(phases, phases_in, sems.at[1]),
        ]
        second = [
            pltpu.make_async_copy(freqs.at[:, at], freqs_in.at[:, at], sems.at[2 + i])
            for i, at in enumerate(spans)
        ]
        third = [
            pltpu.make_async_copy(basis.at[at, :], basis_in.at[at, :], sems.at[2 + blocks + i])
            for i, at in enumerate(spans)
        ]
        for copy in first + second + third:
            copy.start()
        for copy in first:
            copy.wait()
        for copy, at in zip(second, spans):
            copy.wait()
            make_features(points_in, freqs_in, phases_in, feats, parts, at)
        total = None
        for copy, at in zip(third, spans):
            copy.wait()
            value = jnp.dot(parts[:, at], basis_in[at, :], preferred_element_type=F32)
            total = value if total is None else total + value
        coefs[...] = total[:count] + total[count:]

    vmem = pl.BlockSpec(memory_space=pltpu.VMEM)
    hbm = pl.BlockSpec(memory_space=pltpu.HBM)
    return pl.pallas_call(
        kernel,
        in_specs=[hbm] * 4,
        out_specs=[vmem] * 5,
        out_shape=[
            jax.ShapeDtypeStruct((count, width), F32),
            jax.ShapeDtypeStruct((count, rank), F32),
            jax.ShapeDtypeStruct(freqs.shape, freqs.dtype),
            jax.ShapeDtypeStruct(phases.shape, phases.dtype),
            jax.ShapeDtypeStruct(basis.shape, basis.dtype),
        ],
        scratch_shapes=[
            pltpu.VMEM(points.shape, points.dtype),
            pltpu.VMEM((2 * count, width), BF16),
            pltpu.SemaphoreType.DMA((2 + 2 * blocks,)),
        ],
        cost_estimate=COST,
        compiler_params=pltpu.CompilerParams(vmem_limit_bytes=16 << 20),
        name="own_coefs",
    )(*(pltpu.with_memory_space_constraint(x, pltpu.HBM) for x in (points, freqs, phases, basis)))


def other_coefs(place, points, freqs, phases, basis, coefs, block=1024):
    count, width = points.shape[0], freqs.shape[1]

    def kernel(place, points, freqs, phases, basis, coefs, feats, keep, send, parts):
        for start in range(0, width, block):
            make_features(points, freqs, phases, feats, parts, pl.ds(start, block))
        total = jnp.dot(parts[...], basis[...], preferred_element_type=F32)
        others = total[:count] + total[count:]
        keep[...] = jnp.where(place[1] == 0, coefs[...], others)
        send[...] = jnp.where(place[1] == 0, others, coefs[...])

    return on_chip(
        kernel,
        "other_coefs",
        [((count, width), F32), (coefs.shape, F32), (coefs.shape, F32)],
        scalars=1,
        scratch_shapes=[pltpu.VMEM((2 * count, width), BF16)],
    )(place, points, freqs, phases, basis, coefs)


def own_columns(place, own, theirs, passed):
    count, rank = own.shape

    def kernel(place, own, theirs, passed, out):
        other = jnp.where(place[1] == 1, theirs[...], passed[...])
        first = place[0] == 0
        out[:, :rank] = jnp.where(first, own[...], other)
        out[:, rank:] = jnp.where(first, other, own[...])

    return on_chip(kernel, "own_columns", [((count, 2 * rank), F32)], scalars=1)(
        place, own, theirs, passed
    )[0]


def fit_body(place, parts, feats_a, feats_b, basis, fit, left, flip, offset):
    count, size = fit.shape
    half, width = count // 2, basis.shape[0]
    side = 1 - place[0] if flip else place[0]
    at = pl.ds(pl.multiple_of(side * (width // 2) + offset, 128), size)
    value = dot_nt(parts[...], basis[at, :])
    value = value[:count] + value[count:]
    fit[...] = value
    left[:half, :] = feats_b[:, at] - value[half:]
    left[half:, :] = feats_a[:, at] - value[:half]


def first_fit(place, kept, got, feats_a, feats_b, basis, flip, offset, size):
    count, rank = kept.shape

    def kernel(place, kept, got, feats_a, feats_b, basis, fit, left, own, parts):
        first = place[1] == 0
        own[...] = jnp.where(first, kept[...], got[...])
        other = jnp.where(first, got[...], kept[...])
        parts[:count, :], parts[2 * count : 3 * count, :] = split(own[...])
        parts[count : 2 * count, :], parts[3 * count :, :] = split(other)
        fit_body(place, parts, feats_a, feats_b, basis, fit, left, flip, offset)

    return on_chip(
        kernel,
        "first_fit",
        [((2 * count, size), F32)] * 2 + [((count, rank), F32), ((4 * count, rank), BF16)],
        scalars=1,
    )(place, kept, got, feats_a, feats_b, basis)


def fitted(place, parts, feats_a, feats_b, basis, flip, offset, size):
    def kernel(place, parts, feats_a, feats_b, basis, fit, left):
        fit_body(place, parts, feats_a, feats_b, basis, fit, left, flip, offset)

    return on_chip(kernel, "fit", [((parts.shape[0] // 2, size), F32)] * 2, scalars=1)(
        place, parts, feats_a, feats_b, basis
    )


def halves(x):
    return jnp.concatenate(split(x), axis=0)


def overlap(pieces, spans, span):
    start, size = span
    found = []
    for piece, (first, length) in zip(pieces, spans):
        low, high = max(start, first), min(start + size, first + length)
        if low < high:
            found.append((piece, low - first, high - first))
    return [x[0] for x in found], [x[1:] for x in found]


def residual(refs, cuts, got):
    left = [ref[:, low:high] for ref, (low, high) in zip(refs, cuts)]
    return halves(jnp.concatenate(left, axis=1) - got[...])


def add_gram(left, got, total=None):
    pieces, cuts = left
    count, size = got.shape

    def kernel(*refs):
        both = residual(refs, cuts, refs[len(cuts)])
        refs[-2][...] = both
        value = dot_nt(both, both)
        refs[-1][...] = value if total is None else refs[len(cuts) + 1][...] + value

    args = (*pieces, got) if total is None else (*pieces, got, total)
    return on_chip(
        kernel, "gram", [((2 * count, size), BF16), ((2 * count, 2 * count), F32)]
    )(*args)


def gram_halves(place, left, got, total):
    pieces, cuts = left
    count, size = got.shape
    half = count // 2

    def kernel(place, *refs):
        refs, (got, total, parts, keep, send, whole) = refs[:-6], refs[-6:]
        both = residual(refs, cuts, got)
        parts[...] = both
        value = total[...] + dot_nt(both, both)
        whole[...] = (value[:count, :count] + value[count:, count:]) + (
            value[:count, count:] + value[count:, :count]
        )
        ordered = place[0] == 1

        def rows(start):
            value = whole[half_rows(start, half), :]
            swapped = jnp.concatenate([value[:, half:], value[:, :half]], axis=1)
            return jnp.where(ordered, value, swapped)

        mine = jnp.where(ordered, place[1], 1 - place[1])
        keep[...] = rows(mine)
        send[...] = rows(1 - mine)

    return on_chip(
        kernel,
        "gram_halves",
        [((2 * count, size), BF16), ((half, count), F32), ((half, count), F32)],
        scalars=1,
        scratch_shapes=[pltpu.VMEM((count, count), F32)],
    )(place, *pieces, got, total)


def residual_parts(left, got):
    pieces, cuts = left
    count, size = got.shape

    def kernel(*refs):
        refs[-1][...] = residual(refs, cuts, refs[-2])

    return on_chip(kernel, "residual", [((2 * count, size), BF16)])(*pieces, got)[0]


ROWS = 8


def eliminate(matrix):
    size = matrix.shape[0]
    lane = lax.broadcasted_iota(jnp.int32, (ROWS, size), 1)
    row = lax.broadcasted_iota(jnp.int32, (ROWS, size), 0)
    count = size // ROWS
    upper = [matrix[ROWS * i : ROWS * (i + 1), :] for i in range(count)]
    lower = [jnp.where(lane == row + ROWS * i, 1.0, 0.0) for i in range(count)]

    def row_of(x, k):
        return jnp.broadcast_to(x[k : k + 1, :], (ROWS, size))

    def column_of(x, k):
        return jnp.broadcast_to(x[:, k : k + 1], (ROWS, size))

    pivots = []
    for p in range(count):
        columns = [column_of(upper[p], ROWS * p + k) for k in range(ROWS)]
        a, b = upper[p], lower[p]
        inverse, above = [], {}
        pivot = None
        for k in range(ROWS):
            d = row_of(columns[k], k)
            inverse.append(1.0 / d)
            pivot = d if pivot is None else jnp.where(row == k, d, pivot)
            if k < ROWS - 1:
                factor = jnp.where(row > k, columns[k] * inverse[k], 0.0)
                for j in range(k + 1, ROWS):
                    above[k, j] = row_of(columns[j], k)
                    columns[j] = columns[j] - factor * above[k, j]
                a = a - factor * row_of(a, k)
                b = b - factor * row_of(b, k)
        upper[p], lower[p] = a, b
        pivots.append(pivot)
        rows_a = [row_of(a, k) for k in range(ROWS)]
        rows_b = [row_of(b, k) for k in range(ROWS)]
        for i in range(p + 1, count):
            factors = []
            for k in range(ROWS):
                column = column_of(upper[i], ROWS * p + k)
                for j in range(k):
                    column = column - factors[j] * above[j, k]
                factors.append(column * inverse[k])
            for k in range(ROWS):
                upper[i] = upper[i] - factors[k] * rows_a[k]
                lower[i] = lower[i] - factors[k] * rows_b[k]
    return upper, lower, pivots


def factorize(place, kept, got, feats_total):
    half, size = kept.shape

    def kernel(place, kept, got, factor, weights, whole, inverse):
        first = place[1] == 0
        gram = jnp.concatenate(
            [jnp.where(first, kept[...], got[...]), jnp.where(first, got[...], kept[...])], axis=0
        ) * (1.0 / feats_total)
        upper, lower, pivots = eliminate(gram)
        lane = lax.broadcasted_iota(jnp.int32, (ROWS, size), 1)
        row = lax.broadcasted_iota(jnp.int32, (ROWS, size), 0)
        rows = []
        for i, pivot in enumerate(pivots):
            scale = 1.0 / jnp.sqrt(pivot)
            rows.append(jnp.where(lane >= row + ROWS * i, upper[i] * scale, 0.0))
            inverse[ROWS * i : ROWS * (i + 1), :] = lower[i] * scale
        whole[...] = jnp.concatenate(rows, axis=0).T
        factor[...] = whole[half_rows(place[0], half), :]
        own = inverse[half_rows(place[0], half), :]
        swapped = jnp.concatenate([own[:, half:], own[:, :half]], axis=1)
        weights[...] = jnp.where(place[0] == 1, own, swapped)

    return on_chip(
        kernel,
        "factorize",
        [((half, size), F32)] * 2,
        scalars=1,
        cost=LONG,
        scratch_shapes=[pltpu.VMEM((size, size), F32), pltpu.VMEM((size, size), F32)],
    )(place, kept, got)


def new_columns(place, weights, near, far):
    rows = weights.shape[0]
    sizes = [part.shape[1] for part in near + far]
    half = sum(sizes) // 2
    starts = [sum(sizes[:i]) % half for i in range(len(sizes))]

    def kernel(place, weights, *refs):
        parts, (out, whole, sems) = refs[:-3], refs[-3:]
        high, low = split(weights[...])
        lhs = jnp.concatenate(
            [jnp.concatenate([high, high], axis=1), jnp.concatenate([low, low], axis=1)], axis=0
        )
        copies = []
        for index, (start, size) in enumerate(zip(starts, sizes)):
            value = jnp.dot(lhs, parts[index][...], preferred_element_type=F32)
            side = place[0] if index < len(near) else 1 - place[0]
            at = pl.ds(pl.multiple_of(side * half + start, 128), size)
            whole[:, at] = value[:rows] + value[rows:]
            copies.append(pltpu.make_async_copy(whole.at[:, at], out.at[:, at], sems.at[index]))
            copies[-1].start()
        for copy in copies:
            copy.wait()

    vmem = pl.BlockSpec(memory_space=pltpu.VMEM)
    hbm = pl.BlockSpec(memory_space=pltpu.HBM)
    return pl.pallas_call(
        kernel,
        in_specs=[pl.BlockSpec(memory_space=pltpu.SMEM)] + [vmem] * (1 + len(sizes)),
        out_specs=hbm,
        out_shape=jax.ShapeDtypeStruct((rows, 2 * half), F32),
        scratch_shapes=[
            pltpu.VMEM((rows, 2 * half), F32),
            pltpu.SemaphoreType.DMA((len(sizes),)),
        ],
        cost_estimate=COST,
        compiler_params=pltpu.CompilerParams(vmem_limit_bytes=16 << 20),
        name="new_basis",
    )(place, weights, *near, *far)


def swap(x, axis):
    return lax.ppermute(x, axis, [(0, 1), (1, 0)])


def sum_over(x, axis, size):
    terms = [x] + [lax.ppermute(x, axis, [(i, i ^ m) for i in range(size)]) for m in range(1, size)]
    terms = [term.astype(F32) for term in terms]
    while len(terms) > 1:
        terms = [a + b for a, b in zip(terms[::2], terms[1::2])]
    return terms[0]


NEAR = (8, 8, 8, 8)
FAR = (8, 24)


def parted(total, shares):
    cuts = [total * sum(shares[: i + 1]) // sum(shares) // 128 * 128 for i in range(len(shares))]
    return [(start, stop - start) for start, stop in zip([0] + cuts, cuts)]


def paired(feat, feats_total, points, freqs, phases, basis):
    place = jnp.stack([lax.axis_index("pts"), lax.axis_index("sub")]).astype(jnp.int32)
    others = swap(points, "pts")
    feats_a, coefs, freqs, phases, basis = own_coefs(points, freqs, phases[None, :], basis)
    feats_b, keep, send = other_coefs(place, others, freqs, phases, basis, coefs)
    kept = sum_over((keep + swap(send, "sub")).astype(WIRE), "feat", feat)

    half = basis.shape[0] // 2
    near, far = parted(half, NEAR), parted(half, FAR)
    fit, rest, own, parts = first_fit(
        place, kept, swap(kept, "sub"), feats_a, feats_b, basis, 1, *near[0]
    )
    theirs = lax.ppermute(kept, ("pts", "sub"), [(1, 3), (3, 1)])

    def fill(flip, span):
        return fitted(place, parts, feats_a, feats_b, basis, flip, *span)

    fits_away, left_far = zip((fit, rest), *(fill(1, span) for span in near[1:]))
    parts, theirs = lax.optimization_barrier((parts, theirs))
    fits_back, left_near = zip(*(fill(0, span) for span in far))
    fits_away = [fit.astype(WIRE) for fit in fits_away]
    first_back, *fits_back = [fit.astype(WIRE) for fit in fits_back]

    def arrived(fit):
        return swap(fit, "pts").astype(F32)

    got = [arrived(fit) for fit in fits_away]
    total, resids = None, []
    for span, value in zip(near[:-1], got):
        value, total = add_gram(overlap(left_near, far, span), value, total)
        resids.append(value)
    first_got = arrived(first_back)
    total, *fits_back = lax.optimization_barrier((total, *fits_back))
    value, keep, send = gram_halves(place, overlap(left_near, far, near[-1]), got[-1], total)
    resids.append(value)
    gram = keep + swap(send, "sub")
    gram = gram + swap(gram, "pts")
    away = [residual_parts(overlap(left_far, near, far[0]), first_got)]
    gram, away[0], *fits_back = lax.optimization_barrier((gram, away[0], *fits_back))
    away += [
        residual_parts(overlap(left_far, near, span), arrived(fit))
        for span, fit in zip(far[1:], fits_back)
    ]
    gram = sum_over(gram, "feat", feat)
    factor, weights = factorize(place, gram, swap(gram, "sub"), feats_total)
    weights, theirs = lax.optimization_barrier((weights, theirs))
    coefs = own_columns(place, own, theirs, swap(theirs, "sub"))
    coefs, away[-1] = lax.optimization_barrier((coefs, away[-1]))
    new_basis = new_columns(place, weights, resids, away)
    return coefs.T, new_basis.T, factor


def general(feats_total, points, freqs, phases, basis):
    highest = lax.Precision.HIGHEST
    phase_in = jnp.einsum("pd,df->fp", points, freqs, preferred_element_type=F32)
    features = jnp.cos(phase_in + phases[:, None])
    point_cols = features.shape[1]
    whole_basis = lax.all_gather(basis, "pts", axis=1, tiled=True).astype(F32)
    partial_value = jnp.einsum("fk,fp->kp", whole_basis, features, precision=highest)
    coefs = lax.psum(partial_value, ("feat", "sub"))
    residual = features - jnp.dot(whole_basis, coefs, precision=highest)
    spread = lax.all_gather(residual, "pts", axis=1, tiled=True)
    block = jnp.einsum("fq,fp->qp", spread, residual, precision=highest)
    total_pts = block.shape[0]
    block = lax.psum(block, ("feat", "sub")) / feats_total
    gram = lax.all_gather(block, "pts", axis=1, tiled=True)
    factor = jnp.linalg.cholesky(gram)
    inverse = jax.scipy.linalg.solve_triangular(factor, jnp.eye(total_pts, dtype=F32), lower=True)
    offset = lax.axis_index("pts") * point_cols
    factor_rows = lax.dynamic_slice_in_dim(factor, offset, point_cols, 0)
    inv_rows = lax.dynamic_slice_in_dim(inverse, offset, point_cols, 0)
    new_basis = jnp.einsum("fq,pq->fp", spread, inv_rows, precision=highest)
    return coefs, new_basis, factor_rows


def solution(mesh):
    sizes = dict(mesh.shape)
    feat, pts, sub = sizes["feat"], sizes["pts"], sizes["sub"]

    def on_device(points, freqs, phases, basis):
        feats_total = phases.shape[0] * feat * sub
        if pts == 2 and sub == 2 and feat in (1, 2, 4, 8):
            return paired(feat, feats_total, points, freqs, phases, basis)
        return general(feats_total, points, freqs, phases, basis)

    return jax.shard_map(
        on_device,
        mesh=mesh,
        in_specs=(
            P(("groups", "pts"), None),
            P(None, ("feat", "sub")),
            P(("feat", "sub")),
            P(("groups", "feat", "sub"), "pts"),
        ),
        out_specs=(
            P("groups", "pts"),
            P(("groups", "feat", "sub"), "pts"),
            P(("groups", "pts"), None),
        ),
        check_vma=False,
    )
```

```python
import functools

import jax
import jax.numpy as jnp
from jax import lax
from jax.experimental import pallas as pl
from jax.experimental.pallas import tpu as pltpu
from jax.sharding import PartitionSpec as P

BF16, F32, WIRE = jnp.bfloat16, jnp.float32, jnp.float16

COS = (
    0.9999999889369959,
    -0.4999998901135819,
    0.041666488148010265,
    -0.0013887798934755957,
    2.4769791619676175e-05,
    -2.7078195310289617e-07,
    1.7242244242579268e-09,
)
TURN_HEAD = 6.28125
TURN_REST = 0.0019353071795864769


def cosine(x):
    turns = jnp.round(x * 0.15915494309189535)
    x = (x - turns * TURN_HEAD) - turns * TURN_REST
    t = x * x
    y = COS[-1]
    for c in COS[-2::-1]:
        y = y * t + c
    return y


def split(x):
    high = x.astype(BF16)
    return high, (x - high.astype(F32)).astype(BF16)


def dot_nt(a, b):
    return lax.dot_general(a, b, (((1,), (1,)), ((), ())), preferred_element_type=F32)


LONG = pl.CostEstimate(flops=1000, bytes_accessed=20_000_000, transcendentals=0)
COST = pl.CostEstimate(flops=1000, bytes_accessed=1000, transcendentals=0)


def on_chip(kernel, name, out_shape, scalars=0, cost=COST, **extra):
    out_shape = [jax.ShapeDtypeStruct(*out) for out in out_shape]
    vmem = pl.BlockSpec(memory_space=pltpu.VMEM)
    smem = pl.BlockSpec(memory_space=pltpu.SMEM)

    def call(*args):
        return pl.pallas_call(
            kernel,
            in_specs=[smem] * scalars + [vmem] * (len(args) - scalars),
            out_specs=[vmem] * len(out_shape),
            out_shape=out_shape,
            cost_estimate=cost,
            compiler_params=pltpu.CompilerParams(vmem_limit_bytes=16 << 20),
            name=name,
            **extra,
        )(*args)

    return call


def half_rows(index, half):
    return pl.ds(pl.multiple_of(index * half, half), half)


def make_features(points, freqs, phases, feats, parts, at):
    count = points.shape[0]
    x = jnp.dot(points[...], freqs[:, at], preferred_element_type=F32) + phases[:, at]
    value = cosine(x)
    feats[:, at] = value
    parts[:count, at], parts[count:, at] = split(value)


def own_coefs(points, freqs, phases, basis, block=1024):
    count, width, rank = points.shape[0], freqs.shape[1], basis.shape[1]
    blocks = width // block
    spans = [pl.ds(i * block, block) for i in range(blocks)]

    def kernel(points, freqs, phases, basis, feats, coefs, freqs_in, phases_in, basis_in, points_in, parts, sems):
        first = [
            pltpu.make_async_copy(points, points_in, sems.at[0]),
            pltpu.make_async_copy(phases, phases_in, sems.at[1]),
        ]
        second = [
            pltpu.make_async_copy(freqs.at[:, at], freqs_in.at[:, at], sems.at[2 + i])
            for i, at in enumerate(spans)
        ]
        third = [
            pltpu.make_async_copy(basis.at[at, :], basis_in.at[at, :], sems.at[2 + blocks + i])
            for i, at in enumerate(spans)
        ]
        for copy in first + second + third:
            copy.start()
        for copy in first:
            copy.wait()
        for copy, at in zip(second, spans):
            copy.wait()
            make_features(points_in, freqs_in, phases_in, feats, parts, at)
        total = None
        for copy, at in zip(third, spans):
            copy.wait()
            value = jnp.dot(parts[:, at], basis_in[at, :], preferred_element_type=F32)
            total = value if total is None else total + value
        coefs[...] = total[:count] + total[count:]

    vmem = pl.BlockSpec(memory_space=pltpu.VMEM)
    hbm = pl.BlockSpec(memory_space=pltpu.HBM)
    return pl.pallas_call(
        kernel,
        in_specs=[hbm] * 4,
        out_specs=[vmem] * 5,
        out_shape=[
            jax.ShapeDtypeStruct((count, width), F32),
            jax.ShapeDtypeStruct((count, rank), F32),
            jax.ShapeDtypeStruct(freqs.shape, freqs.dtype),
            jax.ShapeDtypeStruct(phases.shape, phases.dtype),
            jax.ShapeDtypeStruct(basis.shape, basis.dtype),
        ],
        scratch_shapes=[
            pltpu.VMEM(points.shape, points.dtype),
            pltpu.VMEM((2 * count, width), BF16),
            pltpu.SemaphoreType.DMA((2 + 2 * blocks,)),
        ],
        cost_estimate=COST,
        compiler_params=pltpu.CompilerParams(vmem_limit_bytes=16 << 20),
        name="own_coefs",
    )(*(pltpu.with_memory_space_constraint(x, pltpu.HBM) for x in (points, freqs, phases, basis)))


def other_coefs(place, points, freqs, phases, basis, coefs, block=1024):
    count, width = points.shape[0], freqs.shape[1]

    def kernel(place, points, freqs, phases, basis, coefs, feats, keep, send, parts):
        for start in range(0, width, block):
            make_features(points, freqs, phases, feats, parts, pl.ds(start, block))
        total = jnp.dot(parts[...], basis[...], preferred_element_type=F32)
        others = total[:count] + total[count:]
        keep[...] = jnp.where(place[1] == 0, coefs[...], others)
        send[...] = jnp.where(place[1] == 0, others, coefs[...])

    return on_chip(
        kernel,
        "other_coefs",
        [((count, width), F32), (coefs.shape, F32), (coefs.shape, F32)],
        scalars=1,
        scratch_shapes=[pltpu.VMEM((2 * count, width), BF16)],
    )(place, points, freqs, phases, basis, coefs)


def own_columns(place, own, theirs, passed):
    count, rank = own.shape

    def kernel(place, own, theirs, passed, out):
        other = jnp.where(place[1] == 1, theirs[...], passed[...])
        first = place[0] == 0
        out[:, :rank] = jnp.where(first, own[...], other)
        out[:, rank:] = jnp.where(first, other, own[...])

    return on_chip(kernel, "own_columns", [((count, 2 * rank), F32)], scalars=1)(
        place, own, theirs, passed
    )[0]


def fit_body(place, parts, feats_a, feats_b, basis, fit, left, flip, offset):
    count, size = fit.shape
    half, width = count // 2, basis.shape[0]
    side = 1 - place[0] if flip else place[0]
    at = pl.ds(pl.multiple_of(side * (width // 2) + offset, 128), size)
    value = dot_nt(parts[...], basis[at, :])
    value = value[:count] + value[count:]
    fit[...] = value
    left[:half, :] = feats_b[:, at] - value[half:]
    left[half:, :] = feats_a[:, at] - value[:half]


def first_fit(place, kept, got, feats_a, feats_b, basis, flip, offset, size):
    count, rank = kept.shape

    def kernel(place, kept, got, feats_a, feats_b, basis, fit, left, own, parts):
        first = place[1] == 0
        own[...] = jnp.where(first, kept[...], got[...])
        other = jnp.where(first, got[...], kept[...])
        parts[:count, :], parts[2 * count : 3 * count, :] = split(own[...])
        parts[count : 2 * count, :], parts[3 * count :, :] = split(other)
        fit_body(place, parts, feats_a, feats_b, basis, fit, left, flip, offset)

    return on_chip(
        kernel,
        "first_fit",
        [((2 * count, size), F32)] * 2 + [((count, rank), F32), ((4 * count, rank), BF16)],
        scalars=1,
    )(place, kept, got, feats_a, feats_b, basis)


def fitted(place, parts, feats_a, feats_b, basis, flip, offset, size):
    def kernel(place, parts, feats_a, feats_b, basis, fit, left):
        fit_body(place, parts, feats_a, feats_b, basis, fit, left, flip, offset)

    return on_chip(kernel, "fit", [((parts.shape[0] // 2, size), F32)] * 2, scalars=1)(
        place, parts, feats_a, feats_b, basis
    )


def halves(x):
    return jnp.concatenate(split(x), axis=0)


def overlap(pieces, spans, span):
    start, size = span
    found = []
    for piece, (first, length) in zip(pieces, spans):
        low, high = max(start, first), min(start + size, first + length)
        if low < high:
            found.append((piece, low - first, high - first))
    return [x[0] for x in found], [x[1:] for x in found]


def residual(refs, cuts, got):
    left = [ref[:, low:high] for ref, (low, high) in zip(refs, cuts)]
    return halves(jnp.concatenate(left, axis=1) - got[...])


def add_gram(left, got, total=None):
    pieces, cuts = left
    count, size = got.shape

    def kernel(*refs):
        both = residual(refs, cuts, refs[len(cuts)])
        refs[-2][...] = both
        value = dot_nt(both, both)
        refs[-1][...] = value if total is None else refs[len(cuts) + 1][...] + value

    args = (*pieces, got) if total is None else (*pieces, got, total)
    return on_chip(
        kernel, "gram", [((2 * count, size), BF16), ((2 * count, 2 * count), F32)]
    )(*args)


def gram_halves(place, left, got, total):
    pieces, cuts = left
    count, size = got.shape
    half = count // 2

    def kernel(place, *refs):
        refs, (got, total, parts, keep, send, whole) = refs[:-6], refs[-6:]
        both = residual(refs, cuts, got)
        parts[...] = both
        value = total[...] + dot_nt(both, both)
        whole[...] = (value[:count, :count] + value[count:, count:]) + (
            value[:count, count:] + value[count:, :count]
        )
        ordered = place[0] == 1

        def rows(start):
            value = whole[half_rows(start, half), :]
            swapped = jnp.concatenate([value[:, half:], value[:, :half]], axis=1)
            return jnp.where(ordered, value, swapped)

        mine = jnp.where(ordered, place[1], 1 - place[1])
        keep[...] = rows(mine)
        send[...] = rows(1 - mine)

    return on_chip(
        kernel,
        "gram_halves",
        [((2 * count, size), BF16), ((half, count), F32), ((half, count), F32)],
        scalars=1,
        scratch_shapes=[pltpu.VMEM((count, count), F32)],
    )(place, *pieces, got, total)


def residual_parts(left, got):
    pieces, cuts = left
    count, size = got.shape

    def kernel(*refs):
        refs[-1][...] = residual(refs, cuts, refs[-2])

    return on_chip(kernel, "residual", [((2 * count, size), BF16)])(*pieces, got)[0]


ROWS = 8


def eliminate(matrix):
    size = matrix.shape[0]
    lane = lax.broadcasted_iota(jnp.int32, (ROWS, size), 1)
    row = lax.broadcasted_iota(jnp.int32, (ROWS, size), 0)
    count = size // ROWS
    upper = [matrix[ROWS * i : ROWS * (i + 1), :] for i in range(count)]
    lower = [jnp.where(lane == row + ROWS * i, 1.0, 0.0) for i in range(count)]

    def row_of(x, k):
        return jnp.broadcast_to(x[k : k + 1, :], (ROWS, size))

    def column_of(x, k):
        return jnp.broadcast_to(x[:, k : k + 1], (ROWS, size))

    pivots = []
    for p in range(count):
        columns = [column_of(upper[p], ROWS * p + k) for k in range(ROWS)]
        a, b = upper[p], lower[p]
        inverse, above = [], {}
        pivot = None
        for k in range(ROWS):
            d = row_of(columns[k], k)
            inverse.append(1.0 / d)
            pivot = d if pivot is None else jnp.where(row == k, d, pivot)
            if k < ROWS - 1:
                factor = jnp.where(row > k, columns[k] * inverse[k], 0.0)
                for j in range(k + 1, ROWS):
                    above[k, j] = row_of(columns[j], k)
                    columns[j] = columns[j] - factor * above[k, j]
                a = a - factor * row_of(a, k)
                b = b - factor * row_of(b, k)
        upper[p], lower[p] = a, b
        pivots.append(pivot)
        rows_a = [row_of(a, k) for k in range(ROWS)]
        rows_b = [row_of(b, k) for k in range(ROWS)]
        for i in range(p + 1, count):
            factors = []
            for k in range(ROWS):
                column = column_of(upper[i], ROWS * p + k)
                for j in range(k):
                    column = column - factors[j] * above[j, k]
                factors.append(column * inverse[k])
            for k in range(ROWS):
                upper[i] = upper[i] - factors[k] * rows_a[k]
                lower[i] = lower[i] - factors[k] * rows_b[k]
    return upper, lower, pivots


def factorize(place, kept, got, feats_total):
    half, size = kept.shape

    def kernel(place, kept, got, factor, weights, whole, inverse):
        first = place[1] == 0
        gram = jnp.concatenate(
            [jnp.where(first, kept[...], got[...]), jnp.where(first, got[...], kept[...])], axis=0
        ) * (1.0 / feats_total)
        upper, lower, pivots = eliminate(gram)
        lane = lax.broadcasted_iota(jnp.int32, (ROWS, size), 1)
        row = lax.broadcasted_iota(jnp.int32, (ROWS, size), 0)
        rows = []
        for i, pivot in enumerate(pivots):
            scale = 1.0 / jnp.sqrt(pivot)
            rows.append(jnp.where(lane >= row + ROWS * i, upper[i] * scale, 0.0))
            inverse[ROWS * i : ROWS * (i + 1), :] = lower[i] * scale
        whole[...] = jnp.concatenate(rows, axis=0).T
        factor[...] = whole[half_rows(place[0], half), :]
        own = inverse[half_rows(place[0], half), :]
        swapped = jnp.concatenate([own[:, half:], own[:, :half]], axis=1)
        weights[...] = jnp.where(place[0] == 1, own, swapped)

    return on_chip(
        kernel,
        "factorize",
        [((half, size), F32)] * 2,
        scalars=1,
        cost=LONG,
        scratch_shapes=[pltpu.VMEM((size, size), F32), pltpu.VMEM((size, size), F32)],
    )(place, kept, got)


def new_columns(place, weights, near, far, left, got):
    rows = weights.shape[0]
    pieces, cuts = left
    half = sum(part.shape[1] for part in near)
    tasks = []
    for flip, group in ((0, near), (1, far + [got])):
        start = 0
        for part in group:
            tasks.append((flip, start, part.shape[1]))
            start += part.shape[1]

    def kernel(place, weights, *refs):
        refs, (out, whole, sems) = refs[:-3], refs[-3:]
        parts, lefts, got = refs[: len(tasks) - 1], refs[len(tasks) - 1 : -1], refs[-1]
        high, low = split(weights[...])
        lhs = jnp.concatenate(
            [jnp.concatenate([high, high], axis=1), jnp.concatenate([low, low], axis=1)], axis=0
        )
        copies = []
        for index, (flip, start, size) in enumerate(tasks):
            part = parts[index][...] if index < len(parts) else residual(lefts, cuts, got)
            value = jnp.dot(lhs, part, preferred_element_type=F32)
            side = 1 - place[0] if flip else place[0]
            at = pl.ds(pl.multiple_of(side * half + start, 128), size)
            whole[:, at] = value[:rows] + value[rows:]
            copies.append(pltpu.make_async_copy(whole.at[:, at], out.at[:, at], sems.at[index]))
            copies[-1].start()
        for copy in copies:
            copy.wait()

    vmem = pl.BlockSpec(memory_space=pltpu.VMEM)
    hbm = pl.BlockSpec(memory_space=pltpu.HBM)
    args = (weights, *near, *far, *pieces, got)
    return pl.pallas_call(
        kernel,
        in_specs=[pl.BlockSpec(memory_space=pltpu.SMEM)] + [vmem] * len(args),
        out_specs=hbm,
        out_shape=jax.ShapeDtypeStruct((rows, 2 * half), F32),
        scratch_shapes=[
            pltpu.VMEM((rows, 2 * half), F32),
            pltpu.SemaphoreType.DMA((len(tasks),)),
        ],
        cost_estimate=COST,
        compiler_params=pltpu.CompilerParams(vmem_limit_bytes=16 << 20),
        name="new_basis",
    )(place, *args)


def swap(x, axis):
    return lax.ppermute(x, axis, [(0, 1), (1, 0)])


def sum_over(x, axis, size):
    terms = [x] + [lax.ppermute(x, axis, [(i, i ^ m) for i in range(size)]) for m in range(1, size)]
    terms = [term.astype(F32) for term in terms]
    while len(terms) > 1:
        terms = [a + b for a, b in zip(terms[::2], terms[1::2])]
    return terms[0]


NEAR = (8, 8, 8, 8)
FAR = (8, 8, 16)


def parted(total, shares):
    cuts = [total * sum(shares[: i + 1]) // sum(shares) // 128 * 128 for i in range(len(shares))]
    return [(start, stop - start) for start, stop in zip([0] + cuts, cuts)]


def paired(feat, feats_total, points, freqs, phases, basis):
    place = jnp.stack([lax.axis_index("pts"), lax.axis_index("sub")]).astype(jnp.int32)
    others = swap(points, "pts")
    feats_a, coefs, freqs, phases, basis = own_coefs(points, freqs, phases[None, :], basis)
    feats_b, keep, send = other_coefs(place, others, freqs, phases, basis, coefs)
    kept = sum_over((keep + swap(send, "sub")).astype(WIRE), "feat", feat)

    half = basis.shape[0] // 2
    near, far = parted(half, NEAR), parted(half, FAR)
    fit, rest, own, parts = first_fit(
        place, kept, swap(kept, "sub"), feats_a, feats_b, basis, 1, *near[0]
    )
    theirs = lax.ppermute(kept, ("pts", "sub"), [(1, 3), (3, 1)])

    def fill(flip, span):
        return fitted(place, parts, feats_a, feats_b, basis, flip, *span)

    fits_away, left_far = zip((fit, rest), *(fill(1, span) for span in near[1:]))
    parts, theirs = lax.optimization_barrier((parts, theirs))
    fits_back, left_near = zip(*(fill(0, span) for span in far))
    fits_away = [fit.astype(WIRE) for fit in fits_away]
    first_back, *fits_back = [fit.astype(WIRE) for fit in fits_back]

    def arrived(fit):
        return swap(fit, "pts").astype(F32)

    got = [arrived(fit) for fit in fits_away]
    total, resids = None, []
    for span, value in zip(near[:-1], got):
        value, total = add_gram(overlap(left_near, far, span), value, total)
        resids.append(value)
    first_got = arrived(first_back)
    total, *fits_back = lax.optimization_barrier((total, *fits_back))
    value, keep, send = gram_halves(place, overlap(left_near, far, near[-1]), got[-1], total)
    resids.append(value)
    gram = keep + swap(send, "sub")
    gram, fits_back[0] = lax.optimization_barrier((gram, fits_back[0]))
    gram = gram + swap(gram, "pts")
    away = [residual_parts(overlap(left_far, near, far[0]), first_got)]
    gram, away[0], *fits_back[1:] = lax.optimization_barrier((gram, away[0], *fits_back[1:]))
    away += [
        residual_parts(overlap(left_far, near, span), arrived(fit))
        for span, fit in zip(far[1:-1], fits_back)
    ]
    last = overlap(left_far, near, far[-1]), arrived(fits_back[-1])
    gram = sum_over(gram, "feat", feat)
    factor, weights = factorize(place, gram, swap(gram, "sub"), feats_total)
    weights, theirs = lax.optimization_barrier((weights, theirs))
    coefs = own_columns(place, own, theirs, swap(theirs, "sub"))
    coefs, away[-1] = lax.optimization_barrier((coefs, away[-1]))
    new_basis = new_columns(place, weights, resids, away, *last)
    return coefs.T, new_basis.T, factor


def general(feats_total, points, freqs, phases, basis):
    highest = lax.Precision.HIGHEST
    phase_in = jnp.einsum("pd,df->fp", points, freqs, preferred_element_type=F32)
    features = jnp.cos(phase_in + phases[:, None])
    point_cols = features.shape[1]
    whole_basis = lax.all_gather(basis, "pts", axis=1, tiled=True).astype(F32)
    partial_value = jnp.einsum("fk,fp->kp", whole_basis, features, precision=highest)
    coefs = lax.psum(partial_value, ("feat", "sub"))
    residual = features - jnp.dot(whole_basis, coefs, precision=highest)
    spread = lax.all_gather(residual, "pts", axis=1, tiled=True)
    block = jnp.einsum("fq,fp->qp", spread, residual, precision=highest)
    total_pts = block.shape[0]
    block = lax.psum(block, ("feat", "sub")) / feats_total
    gram = lax.all_gather(block, "pts", axis=1, tiled=True)
    factor = jnp.linalg.cholesky(gram)
    inverse = jax.scipy.linalg.solve_triangular(factor, jnp.eye(total_pts, dtype=F32), lower=True)
    offset = lax.axis_index("pts") * point_cols
    factor_rows = lax.dynamic_slice_in_dim(factor, offset, point_cols, 0)
    inv_rows = lax.dynamic_slice_in_dim(inverse, offset, point_cols, 0)
    new_basis = jnp.einsum("fq,pq->fp", spread, inv_rows, precision=highest)
    return coefs, new_basis, factor_rows


def solution(mesh):
    sizes = dict(mesh.shape)
    feat, pts, sub = sizes["feat"], sizes["pts"], sizes["sub"]

    def on_device(points, freqs, phases, basis):
        feats_total = phases.shape[0] * feat * sub
        if pts == 2 and sub == 2 and feat in (1, 2, 4, 8):
            return paired(feat, feats_total, points, freqs, phases, basis)
        return general(feats_total, points, freqs, phases, basis)

    return jax.shard_map(
        on_device,
        mesh=mesh,
        in_specs=(
            P(("groups", "pts"), None),
            P(None, ("feat", "sub")),
            P(("feat", "sub")),
            P(("groups", "feat", "sub"), "pts"),
        ),
        out_specs=(
            P("groups", "pts"),
            P(("groups", "feat", "sub"), "pts"),
            P(("groups", "pts"), None),
        ),
        check_vma=False,
    )
```

```python
import functools

import jax
import jax.numpy as jnp
from jax import lax
from jax.experimental import pallas as pl
from jax.experimental.pallas import tpu as pltpu
from jax.sharding import PartitionSpec as P

BF16, F32, WIRE = jnp.bfloat16, jnp.float32, jnp.float16

COS = (
    0.9999999889369959,
    -0.4999998901135819,
    0.041666488148010265,
    -0.0013887798934755957,
    2.4769791619676175e-05,
    -2.7078195310289617e-07,
    1.7242244242579268e-09,
)
TURN_HEAD = 6.28125
TURN_REST = 0.0019353071795864769


def cosine(x):
    turns = jnp.round(x * 0.15915494309189535)
    x = (x - turns * TURN_HEAD) - turns * TURN_REST
    t = x * x
    y = COS[-1]
    for c in COS[-2::-1]:
        y = y * t + c
    return y


def split(x):
    high = x.astype(BF16)
    return high, (x - high.astype(F32)).astype(BF16)


def dot_nt(a, b):
    return lax.dot_general(a, b, (((1,), (1,)), ((), ())), preferred_element_type=F32)


LONG = pl.CostEstimate(flops=1000, bytes_accessed=20_000_000, transcendentals=0)
COST = pl.CostEstimate(flops=1000, bytes_accessed=1000, transcendentals=0)


def on_chip(kernel, name, out_shape, scalars=0, cost=COST, **extra):
    out_shape = [jax.ShapeDtypeStruct(*out) for out in out_shape]
    vmem = pl.BlockSpec(memory_space=pltpu.VMEM)
    smem = pl.BlockSpec(memory_space=pltpu.SMEM)

    def call(*args):
        return pl.pallas_call(
            kernel,
            in_specs=[smem] * scalars + [vmem] * (len(args) - scalars),
            out_specs=[vmem] * len(out_shape),
            out_shape=out_shape,
            cost_estimate=cost,
            compiler_params=pltpu.CompilerParams(vmem_limit_bytes=16 << 20),
            name=name,
            **extra,
        )(*args)

    return call


def half_rows(index, half):
    return pl.ds(pl.multiple_of(index * half, half), half)


def make_features(points, freqs, phases, feats, parts, at):
    count = points.shape[0]
    x = jnp.dot(points[...], freqs[:, at], preferred_element_type=F32) + phases[:, at]
    value = cosine(x)
    feats[:, at] = value
    parts[:count, at], parts[count:, at] = split(value)


def own_coefs(points, freqs, phases, basis, block=1024):
    count, width, rank = points.shape[0], freqs.shape[1], basis.shape[1]
    blocks = width // block
    spans = [pl.ds(i * block, block) for i in range(blocks)]

    def kernel(points, freqs, phases, basis, feats, coefs, freqs_in, phases_in, basis_in, points_in, parts, sems):
        first = [
            pltpu.make_async_copy(points, points_in, sems.at[0]),
            pltpu.make_async_copy(phases, phases_in, sems.at[1]),
        ]
        second = [
            pltpu.make_async_copy(freqs.at[:, at], freqs_in.at[:, at], sems.at[2 + i])
            for i, at in enumerate(spans)
        ]
        third = [
            pltpu.make_async_copy(basis.at[at, :], basis_in.at[at, :], sems.at[2 + blocks + i])
            for i, at in enumerate(spans)
        ]
        for copy in first + second + third:
            copy.start()
        for copy in first:
            copy.wait()
        for copy, at in zip(second, spans):
            copy.wait()
            make_features(points_in, freqs_in, phases_in, feats, parts, at)
        total = None
        for copy, at in zip(third, spans):
            copy.wait()
            value = jnp.dot(parts[:, at], basis_in[at, :], preferred_element_type=F32)
            total = value if total is None else total + value
        coefs[...] = total[:count] + total[count:]

    vmem = pl.BlockSpec(memory_space=pltpu.VMEM)
    hbm = pl.BlockSpec(memory_space=pltpu.HBM)
    return pl.pallas_call(
        kernel,
        in_specs=[hbm] * 4,
        out_specs=[vmem] * 5,
        out_shape=[
            jax.ShapeDtypeStruct((count, width), F32),
            jax.ShapeDtypeStruct((count, rank), F32),
            jax.ShapeDtypeStruct(freqs.shape, freqs.dtype),
            jax.ShapeDtypeStruct(phases.shape, phases.dtype),
            jax.ShapeDtypeStruct(basis.shape, basis.dtype),
        ],
        scratch_shapes=[
            pltpu.VMEM(points.shape, points.dtype),
            pltpu.VMEM((2 * count, width), BF16),
            pltpu.SemaphoreType.DMA((2 + 2 * blocks,)),
        ],
        cost_estimate=COST,
        compiler_params=pltpu.CompilerParams(vmem_limit_bytes=16 << 20),
        name="own_coefs",
    )(*(pltpu.with_memory_space_constraint(x, pltpu.HBM) for x in (points, freqs, phases, basis)))


def other_coefs(place, points, freqs, phases, basis, coefs, block=1024):
    count, width = points.shape[0], freqs.shape[1]

    def kernel(place, points, freqs, phases, basis, coefs, feats, keep, send, parts):
        for start in range(0, width, block):
            make_features(points, freqs, phases, feats, parts, pl.ds(start, block))
        total = jnp.dot(parts[...], basis[...], preferred_element_type=F32)
        others = total[:count] + total[count:]
        keep[...] = jnp.where(place[1] == 0, coefs[...], others)
        send[...] = jnp.where(place[1] == 0, others, coefs[...])

    return on_chip(
        kernel,
        "other_coefs",
        [((count, width), F32), (coefs.shape, F32), (coefs.shape, F32)],
        scalars=1,
        scratch_shapes=[pltpu.VMEM((2 * count, width), BF16)],
    )(place, points, freqs, phases, basis, coefs)


def own_columns(place, own, theirs, passed):
    count, rank = own.shape

    def kernel(place, own, theirs, passed, out):
        other = jnp.where(place[1] == 1, theirs[...], passed[...])
        first = place[0] == 0
        out[:, :rank] = jnp.where(first, own[...], other)
        out[:, rank:] = jnp.where(first, other, own[...])

    return on_chip(kernel, "own_columns", [((count, 2 * rank), F32)], scalars=1)(
        place, own, theirs, passed
    )[0]


def fit_body(place, parts, feats_a, feats_b, basis, fit, left, flip, offset):
    count, size = fit.shape
    half, width = count // 2, basis.shape[0]
    side = 1 - place[0] if flip else place[0]
    at = pl.ds(pl.multiple_of(side * (width // 2) + offset, 128), size)
    value = dot_nt(parts[...], basis[at, :])
    value = value[:count] + value[count:]
    fit[...] = value
    left[:half, :] = feats_b[:, at] - value[half:]
    left[half:, :] = feats_a[:, at] - value[:half]


def first_fit(place, kept, got, feats_a, feats_b, basis, flip, offset, size):
    count, rank = kept.shape

    def kernel(place, kept, got, feats_a, feats_b, basis, fit, left, own, parts):
        first = place[1] == 0
        own[...] = jnp.where(first, kept[...], got[...])
        other = jnp.where(first, got[...], kept[...])
        parts[:count, :], parts[2 * count : 3 * count, :] = split(own[...])
        parts[count : 2 * count, :], parts[3 * count :, :] = split(other)
        fit_body(place, parts, feats_a, feats_b, basis, fit, left, flip, offset)

    return on_chip(
        kernel,
        "first_fit",
        [((2 * count, size), F32)] * 2 + [((count, rank), F32), ((4 * count, rank), BF16)],
        scalars=1,
    )(place, kept, got, feats_a, feats_b, basis)


def fitted(place, parts, feats_a, feats_b, basis, flip, offset, size):
    def kernel(place, parts, feats_a, feats_b, basis, fit, left):
        fit_body(place, parts, feats_a, feats_b, basis, fit, left, flip, offset)

    return on_chip(kernel, "fit", [((parts.shape[0] // 2, size), F32)] * 2, scalars=1)(
        place, parts, feats_a, feats_b, basis
    )


def halves(x):
    return jnp.concatenate(split(x), axis=0)


def overlap(pieces, spans, span):
    start, size = span
    found = []
    for piece, (first, length) in zip(pieces, spans):
        low, high = max(start, first), min(start + size, first + length)
        if low < high:
            found.append((piece, low - first, high - first))
    return [x[0] for x in found], [x[1:] for x in found]


def residual(refs, cuts, got):
    left = [ref[:, low:high] for ref, (low, high) in zip(refs, cuts)]
    return halves(jnp.concatenate(left, axis=1) - got[...])


def residual_span(refs, cuts, got, start, size):
    spans, at = [], 0
    for low, high in cuts:
        spans.append((at, high - low))
        at += high - low
    index, inner = overlap(range(len(refs)), spans, (start, size))
    left = [
        refs[i][:, cuts[i][0] + low : cuts[i][0] + high] for i, (low, high) in zip(index, inner)
    ]
    return halves(jnp.concatenate(left, axis=1) - got[:, start : start + size])


def add_gram(left, got, total=None):
    pieces, cuts = left
    count, size = got.shape

    def kernel(*refs):
        both = residual(refs, cuts, refs[len(cuts)])
        refs[-2][...] = both
        value = dot_nt(both, both)
        refs[-1][...] = value if total is None else refs[len(cuts) + 1][...] + value

    args = (*pieces, got) if total is None else (*pieces, got, total)
    return on_chip(
        kernel, "gram", [((2 * count, size), BF16), ((2 * count, 2 * count), F32)]
    )(*args)


def gram_halves(place, left, got, total):
    pieces, cuts = left
    count, size = got.shape
    half = count // 2

    def kernel(place, *refs):
        refs, (got, total, parts, keep, send, whole) = refs[:-6], refs[-6:]
        both = residual(refs, cuts, got)
        parts[...] = both
        value = total[...] + dot_nt(both, both)
        whole[...] = (value[:count, :count] + value[count:, count:]) + (
            value[:count, count:] + value[count:, :count]
        )
        ordered = place[0] == 1

        def rows(start):
            value = whole[half_rows(start, half), :]
            swapped = jnp.concatenate([value[:, half:], value[:, :half]], axis=1)
            return jnp.where(ordered, value, swapped)

        mine = jnp.where(ordered, place[1], 1 - place[1])
        keep[...] = rows(mine)
        send[...] = rows(1 - mine)

    return on_chip(
        kernel,
        "gram_halves",
        [((2 * count, size), BF16), ((half, count), F32), ((half, count), F32)],
        scalars=1,
        scratch_shapes=[pltpu.VMEM((count, count), F32)],
    )(place, *pieces, got, total)


def residual_parts(left, got):
    pieces, cuts = left
    count, size = got.shape

    def kernel(*refs):
        refs[-1][...] = residual(refs, cuts, refs[-2])

    return on_chip(kernel, "residual", [((2 * count, size), BF16)])(*pieces, got)[0]


ROWS = 8


def eliminate(matrix):
    size = matrix.shape[0]
    lane = lax.broadcasted_iota(jnp.int32, (ROWS, size), 1)
    row = lax.broadcasted_iota(jnp.int32, (ROWS, size), 0)
    count = size // ROWS
    upper = [matrix[ROWS * i : ROWS * (i + 1), :] for i in range(count)]
    lower = [jnp.where(lane == row + ROWS * i, 1.0, 0.0) for i in range(count)]

    def row_of(x, k):
        return jnp.broadcast_to(x[k : k + 1, :], (ROWS, size))

    def column_of(x, k):
        return jnp.broadcast_to(x[:, k : k + 1], (ROWS, size))

    pivots = []
    for p in range(count):
        columns = [column_of(upper[p], ROWS * p + k) for k in range(ROWS)]
        a, b = upper[p], lower[p]
        inverse, above = [], {}
        pivot = None
        for k in range(ROWS):
            d = row_of(columns[k], k)
            inverse.append(1.0 / d)
            pivot = d if pivot is None else jnp.where(row == k, d, pivot)
            if k < ROWS - 1:
                factor = jnp.where(row > k, columns[k] * inverse[k], 0.0)
                for j in range(k + 1, ROWS):
                    above[k, j] = row_of(columns[j], k)
                    columns[j] = columns[j] - factor * above[k, j]
                a = a - factor * row_of(a, k)
                b = b - factor * row_of(b, k)
        upper[p], lower[p] = a, b
        pivots.append(pivot)
        rows_a = [row_of(a, k) for k in range(ROWS)]
        rows_b = [row_of(b, k) for k in range(ROWS)]
        for i in range(p + 1, count):
            factors = []
            for k in range(ROWS):
                column = column_of(upper[i], ROWS * p + k)
                for j in range(k):
                    column = column - factors[j] * above[j, k]
                factors.append(column * inverse[k])
            for k in range(ROWS):
                upper[i] = upper[i] - factors[k] * rows_a[k]
                lower[i] = lower[i] - factors[k] * rows_b[k]
    return upper, lower, pivots


def factorize(place, kept, got, feats_total):
    half, size = kept.shape

    def kernel(place, kept, got, factor, weights, whole, inverse):
        first = place[1] == 0
        gram = jnp.concatenate(
            [jnp.where(first, kept[...], got[...]), jnp.where(first, got[...], kept[...])], axis=0
        ) * (1.0 / feats_total)
        upper, lower, pivots = eliminate(gram)
        lane = lax.broadcasted_iota(jnp.int32, (ROWS, size), 1)
        row = lax.broadcasted_iota(jnp.int32, (ROWS, size), 0)
        rows = []
        for i, pivot in enumerate(pivots):
            scale = 1.0 / jnp.sqrt(pivot)
            rows.append(jnp.where(lane >= row + ROWS * i, upper[i] * scale, 0.0))
            inverse[ROWS * i : ROWS * (i + 1), :] = lower[i] * scale
        whole[...] = jnp.concatenate(rows, axis=0).T
        factor[...] = whole[half_rows(place[0], half), :]
        own = inverse[half_rows(place[0], half), :]
        swapped = jnp.concatenate([own[:, half:], own[:, :half]], axis=1)
        weights[...] = jnp.where(place[0] == 1, own, swapped)

    return on_chip(
        kernel,
        "factorize",
        [((half, size), F32)] * 2,
        scalars=1,
        cost=LONG,
        scratch_shapes=[pltpu.VMEM((size, size), F32), pltpu.VMEM((size, size), F32)],
    )(place, kept, got)


def new_columns(place, weights, near, far, left, got, block=1024):
    rows = weights.shape[0]
    pieces, cuts = left
    half = sum(part.shape[1] for part in near)
    tasks = []
    for flip, group in ((0, near), (1, far + [got])):
        start = 0
        for part in group:
            for low in range(0, part.shape[1], block):
                size = min(block, part.shape[1] - low)
                tasks.append((part is got, len(tasks), low, size, flip, start + low))
            start += part.shape[1]
    parts_of = [index for index, part in enumerate(near + far) for _ in range(0, part.shape[1], block)]

    def kernel(place, weights, *refs):
        refs, (out, whole, sems) = refs[:-3], refs[-3:]
        number = len(near) + len(far)
        parts, lefts, got = refs[:number], refs[number:-1], refs[-1]
        high, low_part = split(weights[...])
        lhs = jnp.concatenate(
            [
                jnp.concatenate([high, high], axis=1),
                jnp.concatenate([low_part, low_part], axis=1),
            ],
            axis=0,
        )
        copies = []
        for is_last, index, low, size, flip, start in tasks:
            if is_last:
                part = residual_span(lefts, cuts, got, low, size)
            else:
                part = parts[parts_of[index]][:, low : low + size]
            value = jnp.dot(lhs, part, preferred_element_type=F32)
            side = 1 - place[0] if flip else place[0]
            at = pl.ds(pl.multiple_of(side * half + start, 128), size)
            whole[:, at] = value[:rows] + value[rows:]
            copies.append(pltpu.make_async_copy(whole.at[:, at], out.at[:, at], sems.at[index]))
            copies[-1].start()
        for copy in copies:
            copy.wait()

    vmem = pl.BlockSpec(memory_space=pltpu.VMEM)
    hbm = pl.BlockSpec(memory_space=pltpu.HBM)
    args = (weights, *near, *far, *pieces, got)
    return pl.pallas_call(
        kernel,
        in_specs=[pl.BlockSpec(memory_space=pltpu.SMEM)] + [vmem] * len(args),
        out_specs=hbm,
        out_shape=jax.ShapeDtypeStruct((rows, 2 * half), F32),
        scratch_shapes=[
            pltpu.VMEM((rows, 2 * half), F32),
            pltpu.SemaphoreType.DMA((len(tasks),)),
        ],
        cost_estimate=COST,
        compiler_params=pltpu.CompilerParams(vmem_limit_bytes=16 << 20),
        name="new_basis",
    )(place, *args)


def swap(x, axis):
    return lax.ppermute(x, axis, [(0, 1), (1, 0)])


def sum_over(x, axis, size):
    terms = [x] + [lax.ppermute(x, axis, [(i, i ^ m) for i in range(size)]) for m in range(1, size)]
    terms = [term.astype(F32) for term in terms]
    while len(terms) > 1:
        terms = [a + b for a, b in zip(terms[::2], terms[1::2])]
    return terms[0]


NEAR = (8, 8, 8, 8)
FAR = (8, 8, 16)


def parted(total, shares):
    cuts = [total * sum(shares[: i + 1]) // sum(shares) // 128 * 128 for i in range(len(shares))]
    return [(start, stop - start) for start, stop in zip([0] + cuts, cuts)]


def paired(feat, feats_total, points, freqs, phases, basis):
    place = jnp.stack([lax.axis_index("pts"), lax.axis_index("sub")]).astype(jnp.int32)
    others = swap(points, "pts")
    feats_a, coefs, freqs, phases, basis = own_coefs(points, freqs, phases[None, :], basis)
    feats_b, keep, send = other_coefs(place, others, freqs, phases, basis, coefs)
    kept = sum_over((keep + swap(send, "sub")).astype(WIRE), "feat", feat)

    half = basis.shape[0] // 2
    near, far = parted(half, NEAR), parted(half, FAR)
    fit, rest, own, parts = first_fit(
        place, kept, swap(kept, "sub"), feats_a, feats_b, basis, 1, *near[0]
    )
    theirs = lax.ppermute(kept, ("pts", "sub"), [(1, 3), (3, 1)])

    def fill(flip, span):
        return fitted(place, parts, feats_a, feats_b, basis, flip, *span)

    fits_away, left_far = zip((fit, rest), *(fill(1, span) for span in near[1:]))
    parts, theirs = lax.optimization_barrier((parts, theirs))
    fits_back, left_near = zip(*(fill(0, span) for span in far))
    fits_away = [fit.astype(WIRE) for fit in fits_away]
    first_back, *fits_back = [fit.astype(WIRE) for fit in fits_back]

    def arrived(fit):
        return swap(fit, "pts").astype(F32)

    got = [arrived(fit) for fit in fits_away]
    total, resids = None, []
    for span, value in zip(near[:-1], got):
        value, total = add_gram(overlap(left_near, far, span), value, total)
        resids.append(value)
    first_got = arrived(first_back)
    total, *fits_back = lax.optimization_barrier((total, *fits_back))
    value, keep, send = gram_halves(place, overlap(left_near, far, near[-1]), got[-1], total)
    resids.append(value)
    gram = keep + swap(send, "sub")
    gram, fits_back[0] = lax.optimization_barrier((gram, fits_back[0]))
    gram = gram + swap(gram, "pts")
    away = [residual_parts(overlap(left_far, near, far[0]), first_got)]
    gram, away[0], *fits_back[1:] = lax.optimization_barrier((gram, away[0], *fits_back[1:]))
    away += [
        residual_parts(overlap(left_far, near, span), arrived(fit))
        for span, fit in zip(far[1:-1], fits_back)
    ]
    last = overlap(left_far, near, far[-1]), arrived(fits_back[-1])
    gram = sum_over(gram, "feat", feat)
    factor, weights = factorize(place, gram, swap(gram, "sub"), feats_total)
    weights, theirs = lax.optimization_barrier((weights, theirs))
    coefs = own_columns(place, own, theirs, swap(theirs, "sub"))
    coefs, away[-1] = lax.optimization_barrier((coefs, away[-1]))
    new_basis = new_columns(place, weights, resids, away, *last)
    return coefs.T, new_basis.T, factor


def general(feats_total, points, freqs, phases, basis):
    highest = lax.Precision.HIGHEST
    phase_in = jnp.einsum("pd,df->fp", points, freqs, preferred_element_type=F32)
    features = jnp.cos(phase_in + phases[:, None])
    point_cols = features.shape[1]
    whole_basis = lax.all_gather(basis, "pts", axis=1, tiled=True).astype(F32)
    partial_value = jnp.einsum("fk,fp->kp", whole_basis, features, precision=highest)
    coefs = lax.psum(partial_value, ("feat", "sub"))
    residual = features - jnp.dot(whole_basis, coefs, precision=highest)
    spread = lax.all_gather(residual, "pts", axis=1, tiled=True)
    block = jnp.einsum("fq,fp->qp", spread, residual, precision=highest)
    total_pts = block.shape[0]
    block = lax.psum(block, ("feat", "sub")) / feats_total
    gram = lax.all_gather(block, "pts", axis=1, tiled=True)
    factor = jnp.linalg.cholesky(gram)
    inverse = jax.scipy.linalg.solve_triangular(factor, jnp.eye(total_pts, dtype=F32), lower=True)
    offset = lax.axis_index("pts") * point_cols
    factor_rows = lax.dynamic_slice_in_dim(factor, offset, point_cols, 0)
    inv_rows = lax.dynamic_slice_in_dim(inverse, offset, point_cols, 0)
    new_basis = jnp.einsum("fq,pq->fp", spread, inv_rows, precision=highest)
    return coefs, new_basis, factor_rows


def solution(mesh):
    sizes = dict(mesh.shape)
    feat, pts, sub = sizes["feat"], sizes["pts"], sizes["sub"]

    def on_device(points, freqs, phases, basis):
        feats_total = phases.shape[0] * feat * sub
        if pts == 2 and sub == 2 and feat in (1, 2, 4, 8):
            return paired(feat, feats_total, points, freqs, phases, basis)
        return general(feats_total, points, freqs, phases, basis)

    return jax.shard_map(
        on_device,
        mesh=mesh,
        in_specs=(
            P(("groups", "pts"), None),
            P(None, ("feat", "sub")),
            P(("feat", "sub")),
            P(("groups", "feat", "sub"), "pts"),
        ),
        out_specs=(
            P("groups", "pts"),
            P(("groups", "feat", "sub"), "pts"),
            P(("groups", "pts"), None),
        ),
        check_vma=False,
    )
```

```python
import functools

import jax
import jax.numpy as jnp
from jax import lax
from jax.experimental import pallas as pl
from jax.experimental.pallas import tpu as pltpu
from jax.sharding import PartitionSpec as P

BF16, F32, WIRE = jnp.bfloat16, jnp.float32, jnp.float16

COS = (
    0.9999999889369959,
    -19.739204464036813,
    64.93911579322743,
    -85.4501108378944,
    60.16740762749498,
    -25.966798028642813,
    6.527580149233599,
)
def cosine(x):
    turns = x * 0.15915494309189535
    t = turns - jnp.round(turns)
    t = t * t
    y = COS[-1]
    for c in COS[-2::-1]:
        y = y * t + c
    return y


def split(x):
    high = x.astype(BF16)
    return high, (x - high.astype(F32)).astype(BF16)


def dot_nt(a, b):
    return lax.dot_general(a, b, (((1,), (1,)), ((), ())), preferred_element_type=F32)


LONG = pl.CostEstimate(flops=1000, bytes_accessed=20_000_000, transcendentals=0)
COST = pl.CostEstimate(flops=1000, bytes_accessed=1000, transcendentals=0)


def on_chip(kernel, name, out_shape, scalars=0, cost=COST, **extra):
    out_shape = [jax.ShapeDtypeStruct(*out) for out in out_shape]
    vmem = pl.BlockSpec(memory_space=pltpu.VMEM)
    smem = pl.BlockSpec(memory_space=pltpu.SMEM)

    def call(*args):
        return pl.pallas_call(
            kernel,
            in_specs=[smem] * scalars + [vmem] * (len(args) - scalars),
            out_specs=[vmem] * len(out_shape),
            out_shape=out_shape,
            cost_estimate=cost,
            compiler_params=pltpu.CompilerParams(vmem_limit_bytes=16 << 20),
            name=name,
            **extra,
        )(*args)

    return call


def half_rows(index, half):
    return pl.ds(pl.multiple_of(index * half, half), half)


def make_features(points, freqs, phases, feats, parts, at):
    count = points.shape[0]
    x = jnp.dot(points[...], freqs[:, at], preferred_element_type=F32) + phases[:, at]
    value = cosine(x)
    feats[:, at] = value
    parts[:count, at], parts[count:, at] = split(value)


def own_coefs(points, freqs, phases, basis, block=1024):
    count, width, rank = points.shape[0], freqs.shape[1], basis.shape[1]
    blocks = width // block
    spans = [pl.ds(i * block, block) for i in range(blocks)]

    def kernel(points, freqs, phases, basis, feats, coefs, freqs_in, phases_in, basis_in, points_in, parts, sems):
        first = [
            pltpu.make_async_copy(points, points_in, sems.at[0]),
            pltpu.make_async_copy(phases, phases_in, sems.at[1]),
        ]
        second = [
            pltpu.make_async_copy(freqs.at[:, at], freqs_in.at[:, at], sems.at[2 + i])
            for i, at in enumerate(spans)
        ]
        third = [
            pltpu.make_async_copy(basis.at[at, :], basis_in.at[at, :], sems.at[2 + blocks + i])
            for i, at in enumerate(spans)
        ]
        for copy in first + second + third:
            copy.start()
        for copy in first:
            copy.wait()
        for copy, at in zip(second, spans):
            copy.wait()
            make_features(points_in, freqs_in, phases_in, feats, parts, at)
        total = None
        for copy, at in zip(third, spans):
            copy.wait()
            value = jnp.dot(parts[:, at], basis_in[at, :], preferred_element_type=F32)
            total = value if total is None else total + value
        coefs[...] = total[:count] + total[count:]

    vmem = pl.BlockSpec(memory_space=pltpu.VMEM)
    hbm = pl.BlockSpec(memory_space=pltpu.HBM)
    return pl.pallas_call(
        kernel,
        in_specs=[hbm] * 4,
        out_specs=[vmem] * 5,
        out_shape=[
            jax.ShapeDtypeStruct((count, width), F32),
            jax.ShapeDtypeStruct((count, rank), F32),
            jax.ShapeDtypeStruct(freqs.shape, freqs.dtype),
            jax.ShapeDtypeStruct(phases.shape, phases.dtype),
            jax.ShapeDtypeStruct(basis.shape, basis.dtype),
        ],
        scratch_shapes=[
            pltpu.VMEM(points.shape, points.dtype),
            pltpu.VMEM((2 * count, width), BF16),
            pltpu.SemaphoreType.DMA((2 + 2 * blocks,)),
        ],
        cost_estimate=COST,
        compiler_params=pltpu.CompilerParams(vmem_limit_bytes=16 << 20),
        name="own_coefs",
    )(*(pltpu.with_memory_space_constraint(x, pltpu.HBM) for x in (points, freqs, phases, basis)))


def other_coefs(place, points, freqs, phases, basis, coefs, block=1024):
    count, width = points.shape[0], freqs.shape[1]

    def kernel(place, points, freqs, phases, basis, coefs, feats, keep, send, parts):
        for start in range(0, width, block):
            make_features(points, freqs, phases, feats, parts, pl.ds(start, block))
        total = jnp.dot(parts[...], basis[...], preferred_element_type=F32)
        others = total[:count] + total[count:]
        keep[...] = jnp.where(place[1] == 0, coefs[...], others)
        send[...] = jnp.where(place[1] == 0, others, coefs[...])

    return on_chip(
        kernel,
        "other_coefs",
        [((count, width), F32), (coefs.shape, F32), (coefs.shape, F32)],
        scalars=1,
        scratch_shapes=[pltpu.VMEM((2 * count, width), BF16)],
    )(place, points, freqs, phases, basis, coefs)


def own_columns(place, own, theirs, passed):
    count, rank = own.shape

    def kernel(place, own, theirs, passed, out):
        other = jnp.where(place[1] == 1, theirs[...], passed[...])
        first = place[0] == 0
        out[:, :rank] = jnp.where(first, own[...], other)
        out[:, rank:] = jnp.where(first, other, own[...])

    return on_chip(kernel, "own_columns", [((count, 2 * rank), F32)], scalars=1)(
        place, own, theirs, passed
    )[0]


def fit_body(place, parts, feats_a, feats_b, basis, fit, left, flip, offset):
    count, size = fit.shape
    half, width = count // 2, basis.shape[0]
    side = 1 - place[0] if flip else place[0]
    at = pl.ds(pl.multiple_of(side * (width // 2) + offset, 128), size)
    value = dot_nt(parts[...], basis[at, :])
    value = value[:count] + value[count:]
    fit[...] = value
    left[:half, :] = feats_b[:, at] - value[half:]
    left[half:, :] = feats_a[:, at] - value[:half]


def first_fit(place, kept, got, feats_a, feats_b, basis, flip, offset, size):
    count, rank = kept.shape

    def kernel(place, kept, got, feats_a, feats_b, basis, fit, left, own, parts):
        first = place[1] == 0
        own[...] = jnp.where(first, kept[...], got[...])
        other = jnp.where(first, got[...], kept[...])
        parts[:count, :], parts[2 * count : 3 * count, :] = split(own[...])
        parts[count : 2 * count, :], parts[3 * count :, :] = split(other)
        fit_body(place, parts, feats_a, feats_b, basis, fit, left, flip, offset)

    return on_chip(
        kernel,
        "first_fit",
        [((2 * count, size), F32)] * 2 + [((count, rank), F32), ((4 * count, rank), BF16)],
        scalars=1,
    )(place, kept, got, feats_a, feats_b, basis)


def fitted(place, parts, feats_a, feats_b, basis, flip, offset, size):
    def kernel(place, parts, feats_a, feats_b, basis, fit, left):
        fit_body(place, parts, feats_a, feats_b, basis, fit, left, flip, offset)

    return on_chip(kernel, "fit", [((parts.shape[0] // 2, size), F32)] * 2, scalars=1)(
        place, parts, feats_a, feats_b, basis
    )


def halves(x):
    return jnp.concatenate(split(x), axis=0)


def overlap(pieces, spans, span):
    start, size = span
    found = []
    for piece, (first, length) in zip(pieces, spans):
        low, high = max(start, first), min(start + size, first + length)
        if low < high:
            found.append((piece, low - first, high - first))
    return [x[0] for x in found], [x[1:] for x in found]


def residual(refs, cuts, got):
    left = [ref[:, low:high] for ref, (low, high) in zip(refs, cuts)]
    return halves(jnp.concatenate(left, axis=1) - got[...])


def add_gram(left, got, total=None):
    pieces, cuts = left
    count, size = got.shape

    def kernel(*refs):
        both = residual(refs, cuts, refs[len(cuts)])
        refs[-2][...] = both
        value = dot_nt(both, both)
        refs[-1][...] = value if total is None else refs[len(cuts) + 1][...] + value

    args = (*pieces, got) if total is None else (*pieces, got, total)
    return on_chip(
        kernel, "gram", [((2 * count, size), BF16), ((2 * count, 2 * count), F32)]
    )(*args)


def gram_halves(place, left, got, total):
    pieces, cuts = left
    count, size = got.shape
    half = count // 2

    def kernel(place, *refs):
        refs, (got, total, parts, keep, send, whole) = refs[:-6], refs[-6:]
        both = residual(refs, cuts, got)
        parts[...] = both
        value = total[...] + dot_nt(both, both)
        whole[...] = (value[:count, :count] + value[count:, count:]) + (
            value[:count, count:] + value[count:, :count]
        )
        ordered = place[0] == 1

        def rows(start):
            value = whole[half_rows(start, half), :]
            swapped = jnp.concatenate([value[:, half:], value[:, :half]], axis=1)
            return jnp.where(ordered, value, swapped)

        mine = jnp.where(ordered, place[1], 1 - place[1])
        keep[...] = rows(mine)
        send[...] = rows(1 - mine)

    return on_chip(
        kernel,
        "gram_halves",
        [((2 * count, size), BF16), ((half, count), F32), ((half, count), F32)],
        scalars=1,
        scratch_shapes=[pltpu.VMEM((count, count), F32)],
    )(place, *pieces, got, total)


def residual_parts(left, got):
    pieces, cuts = left
    count, size = got.shape

    def kernel(*refs):
        refs[-1][...] = residual(refs, cuts, refs[-2])

    return on_chip(kernel, "residual", [((2 * count, size), BF16)])(*pieces, got)[0]


ROWS = 8


def eliminate(matrix):
    size = matrix.shape[0]
    lane = lax.broadcasted_iota(jnp.int32, (ROWS, size), 1)
    row = lax.broadcasted_iota(jnp.int32, (ROWS, size), 0)
    count = size // ROWS
    upper = [matrix[ROWS * i : ROWS * (i + 1), :] for i in range(count)]
    lower = [jnp.where(lane == row + ROWS * i, 1.0, 0.0) for i in range(count)]

    def row_of(x, k):
        return jnp.broadcast_to(x[k : k + 1, :], (ROWS, size))

    def column_of(x, k):
        return jnp.broadcast_to(x[:, k : k + 1], (ROWS, size))

    pivots = []
    for p in range(count):
        columns = [column_of(upper[p], ROWS * p + k) for k in range(ROWS)]
        a, b = upper[p], lower[p]
        inverse, above = [], {}
        pivot = None
        for k in range(ROWS):
            d = row_of(columns[k], k)
            inverse.append(1.0 / d)
            pivot = d if pivot is None else jnp.where(row == k, d, pivot)
            if k < ROWS - 1:
                factor = jnp.where(row > k, columns[k] * inverse[k], 0.0)
                for j in range(k + 1, ROWS):
                    above[k, j] = row_of(columns[j], k)
                    columns[j] = columns[j] - factor * above[k, j]
                a = a - factor * row_of(a, k)
                b = b - factor * row_of(b, k)
        upper[p], lower[p] = a, b
        pivots.append(pivot)
        rows_a = [row_of(a, k) for k in range(ROWS)]
        rows_b = [row_of(b, k) for k in range(ROWS)]
        for i in range(p + 1, count):
            factors = []
            for k in range(ROWS):
                column = column_of(upper[i], ROWS * p + k)
                for j in range(k):
                    column = column - factors[j] * above[j, k]
                factors.append(column * inverse[k])
            for k in range(ROWS):
                upper[i] = upper[i] - factors[k] * rows_a[k]
                lower[i] = lower[i] - factors[k] * rows_b[k]
    return upper, lower, pivots


def factorize(place, kept, got, feats_total):
    half, size = kept.shape

    def kernel(place, kept, got, factor, weights, whole, inverse):
        first = place[1] == 0
        gram = jnp.concatenate(
            [jnp.where(first, kept[...], got[...]), jnp.where(first, got[...], kept[...])], axis=0
        ) * (1.0 / feats_total)
        upper, lower, pivots = eliminate(gram)
        lane = lax.broadcasted_iota(jnp.int32, (ROWS, size), 1)
        row = lax.broadcasted_iota(jnp.int32, (ROWS, size), 0)
        rows = []
        for i, pivot in enumerate(pivots):
            scale = 1.0 / jnp.sqrt(pivot)
            rows.append(jnp.where(lane >= row + ROWS * i, upper[i] * scale, 0.0))
            inverse[ROWS * i : ROWS * (i + 1), :] = lower[i] * scale
        whole[...] = jnp.concatenate(rows, axis=0).T
        factor[...] = whole[half_rows(place[0], half), :]
        own = inverse[half_rows(place[0], half), :]
        swapped = jnp.concatenate([own[:, half:], own[:, :half]], axis=1)
        weights[...] = jnp.where(place[0] == 1, own, swapped)

    return on_chip(
        kernel,
        "factorize",
        [((half, size), F32)] * 2,
        scalars=1,
        cost=LONG,
        scratch_shapes=[pltpu.VMEM((size, size), F32), pltpu.VMEM((size, size), F32)],
    )(place, kept, got)


def new_columns(place, weights, near, far, left, got):
    rows = weights.shape[0]
    pieces, cuts = left
    half = sum(part.shape[1] for part in near)
    tasks = []
    for flip, group in ((0, near), (1, far + [got])):
        start = 0
        for part in group:
            tasks.append((flip, start, part.shape[1]))
            start += part.shape[1]

    def kernel(place, weights, *refs):
        refs, (out, whole, sems) = refs[:-3], refs[-3:]
        parts, lefts, got = refs[: len(tasks) - 1], refs[len(tasks) - 1 : -1], refs[-1]
        high, low = split(weights[...])
        lhs = jnp.concatenate(
            [jnp.concatenate([high, high], axis=1), jnp.concatenate([low, low], axis=1)], axis=0
        )
        copies = []
        for index, (flip, start, size) in enumerate(tasks):
            part = parts[index][...] if index < len(parts) else residual(lefts, cuts, got)
            value = jnp.dot(lhs, part, preferred_element_type=F32)
            side = 1 - place[0] if flip else place[0]
            at = pl.ds(pl.multiple_of(side * half + start, 128), size)
            whole[:, at] = value[:rows] + value[rows:]
            copies.append(pltpu.make_async_copy(whole.at[:, at], out.at[:, at], sems.at[index]))
            copies[-1].start()
        for copy in copies:
            copy.wait()

    vmem = pl.BlockSpec(memory_space=pltpu.VMEM)
    hbm = pl.BlockSpec(memory_space=pltpu.HBM)
    args = (weights, *near, *far, *pieces, got)
    return pl.pallas_call(
        kernel,
        in_specs=[pl.BlockSpec(memory_space=pltpu.SMEM)] + [vmem] * len(args),
        out_specs=hbm,
        out_shape=jax.ShapeDtypeStruct((rows, 2 * half), F32),
        scratch_shapes=[
            pltpu.VMEM((rows, 2 * half), F32),
            pltpu.SemaphoreType.DMA((len(tasks),)),
        ],
        cost_estimate=COST,
        compiler_params=pltpu.CompilerParams(vmem_limit_bytes=16 << 20),
        name="new_basis",
    )(place, *args)


def swap(x, axis):
    return lax.ppermute(x, axis, [(0, 1), (1, 0)])


def sum_over(x, axis, size):
    terms = [x] + [lax.ppermute(x, axis, [(i, i ^ m) for i in range(size)]) for m in range(1, size)]
    terms = [term.astype(F32) for term in terms]
    while len(terms) > 1:
        terms = [a + b for a, b in zip(terms[::2], terms[1::2])]
    return terms[0]


NEAR = (8, 8, 8, 8)
FAR = (8, 8, 16)


def parted(total, shares):
    cuts = [total * sum(shares[: i + 1]) // sum(shares) // 128 * 128 for i in range(len(shares))]
    return [(start, stop - start) for start, stop in zip([0] + cuts, cuts)]


def paired(feat, feats_total, points, freqs, phases, basis):
    place = jnp.stack([lax.axis_index("pts"), lax.axis_index("sub")]).astype(jnp.int32)
    others = swap(points, "pts")
    feats_a, coefs, freqs, phases, basis = own_coefs(points, freqs, phases[None, :], basis)
    feats_b, keep, send = other_coefs(place, others, freqs, phases, basis, coefs)
    kept = sum_over((keep + swap(send, "sub")).astype(WIRE), "feat", feat)

    half = basis.shape[0] // 2
    near, far = parted(half, NEAR), parted(half, FAR)
    fit, rest, own, parts = first_fit(
        place, kept, swap(kept, "sub"), feats_a, feats_b, basis, 1, *near[0]
    )
    theirs = lax.ppermute(kept, ("pts", "sub"), [(1, 3), (3, 1)])

    def fill(flip, span):
        return fitted(place, parts, feats_a, feats_b, basis, flip, *span)

    fits_away, left_far = zip((fit, rest), *(fill(1, span) for span in near[1:]))
    parts, theirs = lax.optimization_barrier((parts, theirs))
    fits_back, left_near = zip(*(fill(0, span) for span in far))
    fits_away = [fit.astype(WIRE) for fit in fits_away]
    first_back, *fits_back = [fit.astype(WIRE) for fit in fits_back]

    def arrived(fit):
        return swap(fit, "pts").astype(F32)

    got = [arrived(fit) for fit in fits_away]
    total, resids = None, []
    for span, value in zip(near[:-1], got):
        value, total = add_gram(overlap(left_near, far, span), value, total)
        resids.append(value)
    first_got = arrived(first_back)
    total, *fits_back = lax.optimization_barrier((total, *fits_back))
    value, keep, send = gram_halves(place, overlap(left_near, far, near[-1]), got[-1], total)
    resids.append(value)
    gram = keep + swap(send, "sub")
    gram, fits_back[0] = lax.optimization_barrier((gram, fits_back[0]))
    gram = gram + swap(gram, "pts")
    away = [residual_parts(overlap(left_far, near, far[0]), first_got)]
    gram, away[0], *fits_back[1:] = lax.optimization_barrier((gram, away[0], *fits_back[1:]))
    away += [
        residual_parts(overlap(left_far, near, span), arrived(fit))
        for span, fit in zip(far[1:-1], fits_back)
    ]
    last = overlap(left_far, near, far[-1]), arrived(fits_back[-1])
    gram = sum_over(gram, "feat", feat)
    factor, weights = factorize(place, gram, swap(gram, "sub"), feats_total)
    weights, theirs = lax.optimization_barrier((weights, theirs))
    coefs = own_columns(place, own, theirs, swap(theirs, "sub"))
    coefs, away[-1] = lax.optimization_barrier((coefs, away[-1]))
    new_basis = new_columns(place, weights, resids, away, *last)
    return coefs.T, new_basis.T, factor


def general(feats_total, points, freqs, phases, basis):
    highest = lax.Precision.HIGHEST
    phase_in = jnp.einsum("pd,df->fp", points, freqs, preferred_element_type=F32)
    features = jnp.cos(phase_in + phases[:, None])
    point_cols = features.shape[1]
    whole_basis = lax.all_gather(basis, "pts", axis=1, tiled=True).astype(F32)
    partial_value = jnp.einsum("fk,fp->kp", whole_basis, features, precision=highest)
    coefs = lax.psum(partial_value, ("feat", "sub"))
    residual = features - jnp.dot(whole_basis, coefs, precision=highest)
    spread = lax.all_gather(residual, "pts", axis=1, tiled=True)
    block = jnp.einsum("fq,fp->qp", spread, residual, precision=highest)
    total_pts = block.shape[0]
    block = lax.psum(block, ("feat", "sub")) / feats_total
    gram = lax.all_gather(block, "pts", axis=1, tiled=True)
    factor = jnp.linalg.cholesky(gram)
    inverse = jax.scipy.linalg.solve_triangular(factor, jnp.eye(total_pts, dtype=F32), lower=True)
    offset = lax.axis_index("pts") * point_cols
    factor_rows = lax.dynamic_slice_in_dim(factor, offset, point_cols, 0)
    inv_rows = lax.dynamic_slice_in_dim(inverse, offset, point_cols, 0)
    new_basis = jnp.einsum("fq,pq->fp", spread, inv_rows, precision=highest)
    return coefs, new_basis, factor_rows


def solution(mesh):
    sizes = dict(mesh.shape)
    feat, pts, sub = sizes["feat"], sizes["pts"], sizes["sub"]

    def on_device(points, freqs, phases, basis):
        feats_total = phases.shape[0] * feat * sub
        if pts == 2 and sub == 2 and feat in (1, 2, 4, 8):
            return paired(feat, feats_total, points, freqs, phases, basis)
        return general(feats_total, points, freqs, phases, basis)

    return jax.shard_map(
        on_device,
        mesh=mesh,
        in_specs=(
            P(("groups", "pts"), None),
            P(None, ("feat", "sub")),
            P(("feat", "sub")),
            P(("groups", "feat", "sub"), "pts"),
        ),
        out_specs=(
            P("groups", "pts"),
            P(("groups", "feat", "sub"), "pts"),
            P(("groups", "pts"), None),
        ),
        check_vma=False,
    )
```

```python
import functools

import jax
import jax.numpy as jnp
from jax import lax
from jax.experimental import pallas as pl
from jax.experimental.pallas import tpu as pltpu
from jax.sharding import PartitionSpec as P

BF16, F32, WIRE = jnp.bfloat16, jnp.float32, jnp.float16

COS = (
    0.9999999889369959,
    -19.739204464036813,
    64.93911579322743,
    -85.4501108378944,
    60.16740762749498,
    -25.966798028642813,
    6.527580149233599,
)
def cosine(x):
    turns = x * 0.15915494309189535
    t = turns - jnp.round(turns)
    t = t * t
    y = COS[-1]
    for c in COS[-2::-1]:
        y = y * t + c
    return y


def split(x):
    high = x.astype(BF16)
    return high, (x - high.astype(F32)).astype(BF16)


def dot_nt(a, b):
    return lax.dot_general(a, b, (((1,), (1,)), ((), ())), preferred_element_type=F32)


LONG = pl.CostEstimate(flops=1000, bytes_accessed=20_000_000, transcendentals=0)
COST = pl.CostEstimate(flops=1000, bytes_accessed=1000, transcendentals=0)


def on_chip(kernel, name, out_shape, scalars=0, cost=COST, **extra):
    out_shape = [jax.ShapeDtypeStruct(*out) for out in out_shape]
    vmem = pl.BlockSpec(memory_space=pltpu.VMEM)
    smem = pl.BlockSpec(memory_space=pltpu.SMEM)

    def call(*args):
        return pl.pallas_call(
            kernel,
            in_specs=[smem] * scalars + [vmem] * (len(args) - scalars),
            out_specs=[vmem] * len(out_shape),
            out_shape=out_shape,
            cost_estimate=cost,
            compiler_params=pltpu.CompilerParams(vmem_limit_bytes=16 << 20),
            name=name,
            **extra,
        )(*args)

    return call


def half_rows(index, half):
    return pl.ds(pl.multiple_of(index * half, half), half)


def make_features(points, freqs, phases, feats, parts, at):
    count = points.shape[0]
    x = jnp.dot(points[...], freqs[:, at], preferred_element_type=F32) + phases[:, at]
    value = cosine(x)
    feats[:, at] = value
    parts[:count, at], parts[count:, at] = split(value)


def own_coefs(points, freqs, phases, basis, block=1024):
    count, width, rank = points.shape[0], freqs.shape[1], basis.shape[1]
    blocks = width // block
    spans = [pl.ds(i * block, block) for i in range(blocks)]

    def kernel(points, freqs, phases, basis, feats, coefs, freqs_in, phases_in, basis_in, points_in, parts, sems):
        first = [
            pltpu.make_async_copy(points, points_in, sems.at[0]),
            pltpu.make_async_copy(phases, phases_in, sems.at[1]),
        ]
        second = [
            pltpu.make_async_copy(freqs.at[:, at], freqs_in.at[:, at], sems.at[2 + i])
            for i, at in enumerate(spans)
        ]
        third = [
            pltpu.make_async_copy(basis.at[at, :], basis_in.at[at, :], sems.at[2 + blocks + i])
            for i, at in enumerate(spans)
        ]
        for copy in first + second + third:
            copy.start()
        for copy in first:
            copy.wait()
        for copy, at in zip(second, spans):
            copy.wait()
            make_features(points_in, freqs_in, phases_in, feats, parts, at)
        total = None
        for copy, at in zip(third, spans):
            copy.wait()
            value = jnp.dot(parts[:, at], basis_in[at, :], preferred_element_type=F32)
            total = value if total is None else total + value
        coefs[...] = total[:count] + total[count:]

    vmem = pl.BlockSpec(memory_space=pltpu.VMEM)
    hbm = pl.BlockSpec(memory_space=pltpu.HBM)
    return pl.pallas_call(
        kernel,
        in_specs=[hbm] * 4,
        out_specs=[vmem] * 5,
        out_shape=[
            jax.ShapeDtypeStruct((count, width), F32),
            jax.ShapeDtypeStruct((count, rank), F32),
            jax.ShapeDtypeStruct(freqs.shape, freqs.dtype),
            jax.ShapeDtypeStruct(phases.shape, phases.dtype),
            jax.ShapeDtypeStruct(basis.shape, basis.dtype),
        ],
        scratch_shapes=[
            pltpu.VMEM(points.shape, points.dtype),
            pltpu.VMEM((2 * count, width), BF16),
            pltpu.SemaphoreType.DMA((2 + 2 * blocks,)),
        ],
        cost_estimate=COST,
        compiler_params=pltpu.CompilerParams(vmem_limit_bytes=16 << 20),
        name="own_coefs",
    )(*(pltpu.with_memory_space_constraint(x, pltpu.HBM) for x in (points, freqs, phases, basis)))


def other_coefs(place, points, freqs, phases, basis, coefs, block=1024):
    count, width = points.shape[0], freqs.shape[1]

    def kernel(place, points, freqs, phases, basis, coefs, feats, keep, send, parts):
        for start in range(0, width, block):
            make_features(points, freqs, phases, feats, parts, pl.ds(start, block))
        total = jnp.dot(parts[...], basis[...], preferred_element_type=F32)
        others = total[:count] + total[count:]
        keep[...] = jnp.where(place[1] == 0, coefs[...], others)
        send[...] = jnp.where(place[1] == 0, others, coefs[...])

    return on_chip(
        kernel,
        "other_coefs",
        [((count, width), F32), (coefs.shape, F32), (coefs.shape, F32)],
        scalars=1,
        scratch_shapes=[pltpu.VMEM((2 * count, width), BF16)],
    )(place, points, freqs, phases, basis, coefs)


def own_columns(place, own, theirs, passed):
    count, rank = own.shape

    def kernel(place, own, theirs, passed, out):
        other = jnp.where(place[1] == 1, theirs[...], passed[...])
        first = place[0] == 0
        out[:, :rank] = jnp.where(first, own[...], other)
        out[:, rank:] = jnp.where(first, other, own[...])

    return on_chip(kernel, "own_columns", [((count, 2 * rank), F32)], scalars=1)(
        place, own, theirs, passed
    )[0]


def fit_body(place, parts, feats_a, feats_b, basis, fit, left, flip, offset):
    count, size = fit.shape
    half, width = count // 2, basis.shape[0]
    side = 1 - place[0] if flip else place[0]
    at = pl.ds(pl.multiple_of(side * (width // 2) + offset, 128), size)
    value = dot_nt(parts[...], basis[at, :])
    value = value[:count] + value[count:]
    fit[...] = value
    left[:half, :] = feats_b[:, at] - value[half:]
    left[half:, :] = feats_a[:, at] - value[:half]


def first_fit(place, kept, got, feats_a, feats_b, basis, flip, offset, size):
    count, rank = kept.shape

    def kernel(place, kept, got, feats_a, feats_b, basis, fit, left, own, parts):
        first = place[1] == 0
        own[...] = jnp.where(first, kept[...], got[...])
        other = jnp.where(first, got[...], kept[...])
        parts[:count, :], parts[2 * count : 3 * count, :] = split(own[...])
        parts[count : 2 * count, :], parts[3 * count :, :] = split(other)
        fit_body(place, parts, feats_a, feats_b, basis, fit, left, flip, offset)

    return on_chip(
        kernel,
        "first_fit",
        [((2 * count, size), F32)] * 2 + [((count, rank), F32), ((4 * count, rank), BF16)],
        scalars=1,
    )(place, kept, got, feats_a, feats_b, basis)


def fitted(place, parts, feats_a, feats_b, basis, flip, offset, size):
    def kernel(place, parts, feats_a, feats_b, basis, fit, left):
        fit_body(place, parts, feats_a, feats_b, basis, fit, left, flip, offset)

    return on_chip(kernel, "fit", [((parts.shape[0] // 2, size), F32)] * 2, scalars=1)(
        place, parts, feats_a, feats_b, basis
    )


def halves(x):
    return jnp.concatenate(split(x), axis=0)


def overlap(pieces, spans, span):
    start, size = span
    found = []
    for piece, (first, length) in zip(pieces, spans):
        low, high = max(start, first), min(start + size, first + length)
        if low < high:
            found.append((piece, low - first, high - first))
    return [x[0] for x in found], [x[1:] for x in found]


def residual(refs, cuts, got):
    left = [ref[:, low:high] for ref, (low, high) in zip(refs, cuts)]
    return halves(jnp.concatenate(left, axis=1) - got[...])


def residual_span(refs, cuts, got, start, size):
    spans, at = [], 0
    for low, high in cuts:
        spans.append((at, high - low))
        at += high - low
    index, inner = overlap(range(len(refs)), spans, (start, size))
    left = [
        refs[i][:, cuts[i][0] + low : cuts[i][0] + high] for i, (low, high) in zip(index, inner)
    ]
    return halves(jnp.concatenate(left, axis=1) - got[:, start : start + size])


def add_gram(left, got, total=None):
    pieces, cuts = left
    count, size = got.shape

    def kernel(*refs):
        both = residual(refs, cuts, refs[len(cuts)])
        refs[-2][...] = both
        value = dot_nt(both, both)
        refs[-1][...] = value if total is None else refs[len(cuts) + 1][...] + value

    args = (*pieces, got) if total is None else (*pieces, got, total)
    return on_chip(
        kernel, "gram", [((2 * count, size), BF16), ((2 * count, 2 * count), F32)]
    )(*args)


def gram_halves(place, left, got, total):
    pieces, cuts = left
    count, size = got.shape
    half = count // 2

    def kernel(place, *refs):
        refs, (got, total, parts, keep, send, whole) = refs[:-6], refs[-6:]
        both = residual(refs, cuts, got)
        parts[...] = both
        value = total[...] + dot_nt(both, both)
        whole[...] = (value[:count, :count] + value[count:, count:]) + (
            value[:count, count:] + value[count:, :count]
        )
        ordered = place[0] == 1

        def rows(start):
            value = whole[half_rows(start, half), :]
            swapped = jnp.concatenate([value[:, half:], value[:, :half]], axis=1)
            return jnp.where(ordered, value, swapped)

        mine = jnp.where(ordered, place[1], 1 - place[1])
        keep[...] = rows(mine)
        send[...] = rows(1 - mine)

    return on_chip(
        kernel,
        "gram_halves",
        [((2 * count, size), BF16), ((half, count), F32), ((half, count), F32)],
        scalars=1,
        scratch_shapes=[pltpu.VMEM((count, count), F32)],
    )(place, *pieces, got, total)


def residual_parts(left, got):
    pieces, cuts = left
    count, size = got.shape

    def kernel(*refs):
        refs[-1][...] = residual(refs, cuts, refs[-2])

    return on_chip(kernel, "residual", [((2 * count, size), BF16)])(*pieces, got)[0]


ROWS = 8


def eliminate(matrix):
    size = matrix.shape[0]
    lane = lax.broadcasted_iota(jnp.int32, (ROWS, size), 1)
    row = lax.broadcasted_iota(jnp.int32, (ROWS, size), 0)
    count = size // ROWS
    upper = [matrix[ROWS * i : ROWS * (i + 1), :] for i in range(count)]
    lower = [jnp.where(lane == row + ROWS * i, 1.0, 0.0) for i in range(count)]

    def row_of(x, k):
        return jnp.broadcast_to(x[k : k + 1, :], (ROWS, size))

    def column_of(x, k):
        return jnp.broadcast_to(x[:, k : k + 1], (ROWS, size))

    pivots = []
    for p in range(count):
        columns = [column_of(upper[p], ROWS * p + k) for k in range(ROWS)]
        a, b = upper[p], lower[p]
        inverse, above = [], {}
        pivot = None
        for k in range(ROWS):
            d = row_of(columns[k], k)
            inverse.append(1.0 / d)
            pivot = d if pivot is None else jnp.where(row == k, d, pivot)
            if k < ROWS - 1:
                factor = jnp.where(row > k, columns[k] * inverse[k], 0.0)
                for j in range(k + 1, ROWS):
                    above[k, j] = row_of(columns[j], k)
                    columns[j] = columns[j] - factor * above[k, j]
                a = a - factor * row_of(a, k)
                b = b - factor * row_of(b, k)
        upper[p], lower[p] = a, b
        pivots.append(pivot)
        rows_a = [row_of(a, k) for k in range(ROWS)]
        rows_b = [row_of(b, k) for k in range(ROWS)]
        for i in range(p + 1, count):
            factors = []
            for k in range(ROWS):
                column = column_of(upper[i], ROWS * p + k)
                for j in range(k):
                    column = column - factors[j] * above[j, k]
                factors.append(column * inverse[k])
            for k in range(ROWS):
                upper[i] = upper[i] - factors[k] * rows_a[k]
                lower[i] = lower[i] - factors[k] * rows_b[k]
    return upper, lower, pivots


def factorize(place, kept, got, feats_total):
    half, size = kept.shape

    def kernel(place, kept, got, factor, weights, whole, inverse):
        first = place[1] == 0
        gram = jnp.concatenate(
            [jnp.where(first, kept[...], got[...]), jnp.where(first, got[...], kept[...])], axis=0
        ) * (1.0 / feats_total)
        upper, lower, pivots = eliminate(gram)
        lane = lax.broadcasted_iota(jnp.int32, (ROWS, size), 1)
        row = lax.broadcasted_iota(jnp.int32, (ROWS, size), 0)
        rows = []
        for i, pivot in enumerate(pivots):
            scale = 1.0 / jnp.sqrt(pivot)
            rows.append(jnp.where(lane >= row + ROWS * i, upper[i] * scale, 0.0))
            inverse[ROWS * i : ROWS * (i + 1), :] = lower[i] * scale
        whole[...] = jnp.concatenate(rows, axis=0).T
        factor[...] = whole[half_rows(place[0], half), :]
        own = inverse[half_rows(place[0], half), :]
        swapped = jnp.concatenate([own[:, half:], own[:, :half]], axis=1)
        weights[...] = jnp.where(place[0] == 1, own, swapped)

    return on_chip(
        kernel,
        "factorize",
        [((half, size), F32)] * 2,
        scalars=1,
        cost=LONG,
        scratch_shapes=[pltpu.VMEM((size, size), F32), pltpu.VMEM((size, size), F32)],
    )(place, kept, got)


def new_columns(place, weights, near, far, left, got, block=1024):
    rows = weights.shape[0]
    pieces, cuts = left
    half = sum(part.shape[1] for part in near)
    tasks = []
    for flip, group in ((0, near), (1, far + [got])):
        start = 0
        for part in group:
            for low in range(0, part.shape[1], block):
                size = min(block, part.shape[1] - low)
                tasks.append((part is got, len(tasks), low, size, flip, start + low))
            start += part.shape[1]
    parts_of = [index for index, part in enumerate(near + far) for _ in range(0, part.shape[1], block)]

    def kernel(place, weights, *refs):
        refs, (out, whole, sems) = refs[:-3], refs[-3:]
        number = len(near) + len(far)
        parts, lefts, got = refs[:number], refs[number:-1], refs[-1]
        high, low_part = split(weights[...])
        lhs = jnp.concatenate(
            [
                jnp.concatenate([high, high], axis=1),
                jnp.concatenate([low_part, low_part], axis=1),
            ],
            axis=0,
        )
        copies = []
        for is_last, index, low, size, flip, start in tasks:
            if is_last:
                part = residual_span(lefts, cuts, got, low, size)
            else:
                part = parts[parts_of[index]][:, low : low + size]
            value = jnp.dot(lhs, part, preferred_element_type=F32)
            side = 1 - place[0] if flip else place[0]
            at = pl.ds(pl.multiple_of(side * half + start, 128), size)
            whole[:, at] = value[:rows] + value[rows:]
            copies.append(pltpu.make_async_copy(whole.at[:, at], out.at[:, at], sems.at[index]))
            copies[-1].start()
        for copy in copies:
            copy.wait()

    vmem = pl.BlockSpec(memory_space=pltpu.VMEM)
    hbm = pl.BlockSpec(memory_space=pltpu.HBM)
    args = (weights, *near, *far, *pieces, got)
    return pl.pallas_call(
        kernel,
        in_specs=[pl.BlockSpec(memory_space=pltpu.SMEM)] + [vmem] * len(args),
        out_specs=hbm,
        out_shape=jax.ShapeDtypeStruct((rows, 2 * half), F32),
        scratch_shapes=[
            pltpu.VMEM((rows, 2 * half), F32),
            pltpu.SemaphoreType.DMA((len(tasks),)),
        ],
        cost_estimate=COST,
        compiler_params=pltpu.CompilerParams(vmem_limit_bytes=16 << 20),
        name="new_basis",
    )(place, *args)


def swap(x, axis):
    return lax.ppermute(x, axis, [(0, 1), (1, 0)])


def sum_over(x, axis, size):
    terms = [x] + [lax.ppermute(x, axis, [(i, i ^ m) for i in range(size)]) for m in range(1, size)]
    terms = [term.astype(F32) for term in terms]
    while len(terms) > 1:
        terms = [a + b for a, b in zip(terms[::2], terms[1::2])]
    return terms[0]


NEAR = (8, 8, 8, 8)
FAR = (8, 8, 16)


def parted(total, shares):
    cuts = [total * sum(shares[: i + 1]) // sum(shares) // 128 * 128 for i in range(len(shares))]
    return [(start, stop - start) for start, stop in zip([0] + cuts, cuts)]


def paired(feat, feats_total, points, freqs, phases, basis):
    place = jnp.stack([lax.axis_index("pts"), lax.axis_index("sub")]).astype(jnp.int32)
    others = swap(points, "pts")
    feats_a, coefs, freqs, phases, basis = own_coefs(points, freqs, phases[None, :], basis)
    feats_b, keep, send = other_coefs(place, others, freqs, phases, basis, coefs)
    kept = sum_over((keep + swap(send, "sub")).astype(WIRE), "feat", feat)

    half = basis.shape[0] // 2
    near, far = parted(half, NEAR), parted(half, FAR)
    fit, rest, own, parts = first_fit(
        place, kept, swap(kept, "sub"), feats_a, feats_b, basis, 1, *near[0]
    )
    theirs = lax.ppermute(kept, ("pts", "sub"), [(1, 3), (3, 1)])

    def fill(flip, span):
        return fitted(place, parts, feats_a, feats_b, basis, flip, *span)

    fits_away, left_far = zip((fit, rest), *(fill(1, span) for span in near[1:]))
    parts, theirs = lax.optimization_barrier((parts, theirs))
    fits_back, left_near = zip(*(fill(0, span) for span in far))
    fits_away = [fit.astype(WIRE) for fit in fits_away]
    first_back, *fits_back = [fit.astype(WIRE) for fit in fits_back]

    def arrived(fit):
        return swap(fit, "pts").astype(F32)

    got = [arrived(fit) for fit in fits_away]
    total, resids = None, []
    for span, value in zip(near[:-1], got):
        value, total = add_gram(overlap(left_near, far, span), value, total)
        resids.append(value)
    first_got = arrived(first_back)
    total, *fits_back = lax.optimization_barrier((total, *fits_back))
    value, keep, send = gram_halves(place, overlap(left_near, far, near[-1]), got[-1], total)
    resids.append(value)
    gram = keep + swap(send, "sub")
    gram, fits_back[0] = lax.optimization_barrier((gram, fits_back[0]))
    gram = gram + swap(gram, "pts")
    away = [residual_parts(overlap(left_far, near, far[0]), first_got)]
    gram, away[0], *fits_back[1:] = lax.optimization_barrier((gram, away[0], *fits_back[1:]))
    away += [
        residual_parts(overlap(left_far, near, span), arrived(fit))
        for span, fit in zip(far[1:-1], fits_back)
    ]
    last = overlap(left_far, near, far[-1]), arrived(fits_back[-1])
    gram = sum_over(gram, "feat", feat)
    factor, weights = factorize(place, gram, swap(gram, "sub"), feats_total)
    weights, theirs = lax.optimization_barrier((weights, theirs))
    coefs = own_columns(place, own, theirs, swap(theirs, "sub"))
    coefs, away[-1] = lax.optimization_barrier((coefs, away[-1]))
    new_basis = new_columns(place, weights, resids, away, *last)
    return coefs.T, new_basis.T, factor


def general(feats_total, points, freqs, phases, basis):
    highest = lax.Precision.HIGHEST
    phase_in = jnp.einsum("pd,df->fp", points, freqs, preferred_element_type=F32)
    features = jnp.cos(phase_in + phases[:, None])
    point_cols = features.shape[1]
    whole_basis = lax.all_gather(basis, "pts", axis=1, tiled=True).astype(F32)
    partial_value = jnp.einsum("fk,fp->kp", whole_basis, features, precision=highest)
    coefs = lax.psum(partial_value, ("feat", "sub"))
    residual = features - jnp.dot(whole_basis, coefs, precision=highest)
    spread = lax.all_gather(residual, "pts", axis=1, tiled=True)
    block = jnp.einsum("fq,fp->qp", spread, residual, precision=highest)
    total_pts = block.shape[0]
    block = lax.psum(block, ("feat", "sub")) / feats_total
    gram = lax.all_gather(block, "pts", axis=1, tiled=True)
    factor = jnp.linalg.cholesky(gram)
    inverse = jax.scipy.linalg.solve_triangular(factor, jnp.eye(total_pts, dtype=F32), lower=True)
    offset = lax.axis_index("pts") * point_cols
    factor_rows = lax.dynamic_slice_in_dim(factor, offset, point_cols, 0)
    inv_rows = lax.dynamic_slice_in_dim(inverse, offset, point_cols, 0)
    new_basis = jnp.einsum("fq,pq->fp", spread, inv_rows, precision=highest)
    return coefs, new_basis, factor_rows


def solution(mesh):
    sizes = dict(mesh.shape)
    feat, pts, sub = sizes["feat"], sizes["pts"], sizes["sub"]

    def on_device(points, freqs, phases, basis):
        feats_total = phases.shape[0] * feat * sub
        if pts == 2 and sub == 2 and feat in (1, 2, 4, 8):
            return paired(feat, feats_total, points, freqs, phases, basis)
        return general(feats_total, points, freqs, phases, basis)

    return jax.shard_map(
        on_device,
        mesh=mesh,
        in_specs=(
            P(("groups", "pts"), None),
            P(None, ("feat", "sub")),
            P(("feat", "sub")),
            P(("groups", "feat", "sub"), "pts"),
        ),
        out_specs=(
            P("groups", "pts"),
            P(("groups", "feat", "sub"), "pts"),
            P(("groups", "pts"), None),
        ),
        check_vma=False,
    )
```
